256 devices in a mesh: seq: 32 (over z, y), head: 8 (over x, core).
Axes of the slice: x: 4, y: 4, z: 8, core: 2. Of those that a mesh axis runs over, the one named last changes fastest.
Arguments:
- queries: bfloat16 [16384, 8192], P('seq', 'head'), may hold values from -6 to 6
- keys: bfloat16 [16384, 8192], P('seq', 'head'), may hold values from -6 to 6
- values: bfloat16 [16384, 8192], P('seq', 'head'), may hold values from -120 to 120
- gate: bfloat16 [16384, 8192], P('seq', 'head'), may hold values from -6 to 6
- grad_out: bfloat16 [16384, 8192], P('seq', 'head'), may hold values from -6 to 6
- gain: float32 [8192], P('head'), may hold values from 0.25 to 1.75
- tile_mask: int32 [128, 4], P('seq'), may hold values from 0 to 1, as said below
Outputs:
- grad_queries: bfloat16 [16384, 8192], P('seq', 'head')
- grad_keys: bfloat16 [16384, 8192], P('seq', 'head')
- grad_values: bfloat16 [16384, 8192], P('seq', 'head')
- grad_gate: bfloat16 [16384, 8192], P('seq', 'head')
- grad_gain: float32 [8192], P('head')
The draws below stay inside these ranges and needn't reach their ends.
Inputs may be any that keep to these rules, and one draw needn't show every extreme that they name: `tile_mask`: entries are 0 or 1; in every slab's 4 x 4 block the diagonal is 1 and entries above it are 0.
All inputs are finite; a program needn't handle non-finite values.
Results may differ from the reference program's by a relative error of at most 0.0058.
Values sent between devices are 32-bit elements; how exact they have to be, the bound alone decides.
A program may use at most 128 MiB of HBM per device.

```python
import jax
import jax.numpy as jnp
from jax import lax

HEADS = 64
HD = 128
TOK_DEV = 512
TILE = 128
TILES = 4
SLABS = 32
TOKENS = 16384
D = 8192


def draw_values(key, part):
    first, second = jax.random.split(key)
    column_head = (jnp.arange(HEADS * HD) // HD).astype(jnp.float32)
    spread = jax.random.uniform(second, (HEADS * HD,), jnp.float32)
    scale = 3.0 ** (column_head / max(HEADS - 1, 1)) * 10.0 ** spread
    base = jax.random.truncated_normal(first, -4.0, 4.0, (TOKENS, HEADS * HD), jnp.float32)
    return (base * scale[None, :]).astype(jnp.bfloat16)


def draw_tile_mask(key, part):
    picks = jax.random.randint(key, (SLABS * TILES, TILES), 0, 10)
    ones = (picks < 7).astype(jnp.int32)
    row_tile = (jnp.arange(SLABS * TILES) % TILES)[:, None]
    col_tile = jnp.arange(TILES)[None, :]
    lower = col_tile < row_tile
    diagonal = col_tile == row_tile
    return jnp.where(diagonal, 1, jnp.where(lower, ones, 0)).astype(jnp.int32)


def level_of(own_key, shape, cuts, least, largest):
    loudness, own = 1.0, jax.random.fold_in(own_key, 6)
    for axis_at, parts in cuts:
        draws = jnp.exp(jax.random.uniform(jax.random.fold_in(own, axis_at), (parts,), jnp.float32, least / len(cuts), largest / len(cuts)))
        loudness = loudness * jnp.repeat(draws, shape[axis_at] // parts).reshape([-1 if axis == axis_at else 1 for axis in range(len(shape))])
    return loudness


def normal_values(rng, extent, deviation, limit, shards=(), kind=jnp.bfloat16):
    entries = deviation * jax.random.normal(rng, extent, jnp.float32)
    if shards:
        entries = entries * level_of(rng, extent, shards, -0.22, 0.18)
    return jnp.clip(entries, -limit, limit).astype(kind)


def setup_inputs(seed: int = 0) -> dict:
    splits = jax.random.split(jax.random.key(seed), 8)
    return {
        "queries": normal_values(splits[0], (TOKENS, D), 1.0, 6.0, ((0, 32), (1, 8))),
        "keys": normal_values(splits[1], (TOKENS, D), 1.0, 6.0, ((0, 32), (1, 8))),
        "values": draw_values(jax.random.fold_in(splits[7], 71), 0),
        "gate": normal_values(splits[3], (TOKENS, D), 1.5, 6.0, ((0, 32), (1, 8))),
        "grad_out": normal_values(splits[4], (TOKENS, D), 1.0, 6.0, ((0, 32), (1, 8))),
        "gain": jnp.clip(1.0 + 0.15 * jax.random.normal(splits[5], (D,), jnp.float32), 0.25, 1.75),
        "tile_mask": draw_tile_mask(jax.random.fold_in(splits[7], 71), 0),
    }


def round_half(x):
    return lax.optimization_barrier(x.astype(jnp.bfloat16)).astype(jnp.float32)

def keep_mask(tile_rows):
    tiles = tile_rows.shape[0]
    expand = jnp.broadcast_to(tile_rows[:, None, :, None], (tiles, TILE, tiles, TILE)).reshape(TOK_DEV, TOK_DEV) == 1
    place = jnp.arange(TOK_DEV)
    same = place[:, None] // TILE == place[None, :] // TILE
    causal = place[:, None] >= place[None, :]
    return expand & (causal | jnp.logical_not(same))

def reference(queries, keys, values, gate, grad_out, gain, tile_mask):
    f = jnp.float32
    q = queries.astype(f).reshape(SLABS, TOK_DEV, HEADS, HD)
    k = keys.astype(f).reshape(SLABS, TOK_DEV, HEADS, HD)
    v = values.astype(f).reshape(SLABS, TOK_DEV, HEADS, HD)
    masks = tile_mask.reshape(SLABS, TILES, TILES)
    local = jnp.einsum('sthe,sthf->shef', k, v)
    running = jnp.cumsum(local, 0)
    prefix = round_half(jnp.concatenate([jnp.zeros((1, HEADS, HD, HD), f), running[:-1]], 0))

    def forward(item):
        qs, ks, vs, ms, ps = item
        keep = keep_mask(ms)
        scores = jnp.einsum('the,she->hts', qs, ks)
        probs = round_half(jnp.where(keep[None], scores, 0.0))
        return jnp.einsum('hts,shf->thf', probs, vs) + jnp.einsum('the,hef->thf', qs, ps)
    attn = lax.map(forward, (q, k, v, masks, prefix)).reshape(TOKENS, D)
    ms_rows = lax.optimization_barrier(jnp.mean(attn * attn, -1, keepdims=True))
    rms = jnp.sqrt(ms_rows + 1e-06)
    normed = attn / rms
    sig = jax.nn.sigmoid(gate.astype(f))
    upstream = grad_out.astype(f)
    dnorm = upstream * sig
    grad_gate = (upstream * normed * gain * sig * (1.0 - sig)).astype(jnp.bfloat16)
    grad_gain = lax.optimization_barrier(jnp.sum(dnorm * normed, 0))
    cross = lax.optimization_barrier(jnp.mean(dnorm * gain * attn, -1, keepdims=True))
    dattn = round_half((dnorm * gain - attn * cross / (ms_rows + 1e-06)) / rms)
    da = dattn.reshape(SLABS, TOK_DEV, HEADS, HD)
    local_adj = jnp.einsum('sthe,sthf->shef', q, da)
    back = jnp.cumsum(local_adj[::-1], 0)[::-1]
    suffix = round_half(jnp.concatenate([back[1:], jnp.zeros((1, HEADS, HD, HD), f)], 0))

    def backward(item):
        qs, ks, vs, das, ms, ps, ss = item
        keep = keep_mask(ms)
        probs = round_half(jnp.where(keep[None], jnp.einsum('the,she->hts', qs, ks), 0.0))
        dprobs = round_half(jnp.where(keep[None], jnp.einsum('thf,shf->hts', das, vs), 0.0))
        gq = jnp.einsum('hts,she->the', dprobs, ks) + jnp.einsum('thf,hef->the', das, ps)
        gk = jnp.einsum('hts,the->she', dprobs, qs) + jnp.einsum('shf,hef->she', vs, ss)
        gv = jnp.einsum('hts,thf->shf', probs, das) + jnp.einsum('she,hef->shf', ks, ss)
        return (gq.astype(jnp.bfloat16), gk.astype(jnp.bfloat16), gv.astype(jnp.bfloat16))
    gq, gk, gv = lax.map(backward, (q, k, v, da, masks, prefix, suffix))
    return (gq.reshape(TOKENS, D), gk.reshape(TOKENS, D), gv.reshape(TOKENS, D), grad_gate, grad_gain)
```

```python
import functools

import jax
import jax.numpy as jnp
from jax import lax
from jax.experimental import pallas as pl
from jax.experimental.pallas import tpu as pltpu
from jax.sharding import PartitionSpec as P

HD = 128
TILE = 128
NY = 4
CHUNKS = 4
MESH = pl.DeviceIdType.MESH
F32 = jnp.float32
BF = jnp.bfloat16


def dot(a, b):
    return lax.dot_general(a, b, (((1,), (0,)), ((), ())), preferred_element_type=F32)


def dot_nt(a, b):
    return lax.dot_general(a, b, (((1,), (1,)), ((), ())), preferred_element_type=F32)


def dot_tn(a, b):
    return lax.dot_general(a, b, (((0,), (0,)), ((), ())), preferred_element_type=F32)


def each(lo, hi, fn):
    def step(i, carry):
        fn(i)
        return carry

    lax.fori_loop(lo, hi, step, 0)


def layer_kernel(
    nz,
    nh,
    heads,
    rows,
    full,
    q_hbm,
    k_hbm,
    v_hbm,
    gate_hbm,
    go_hbm,
    gain_ref,
    tm_ref,
    gq_hbm,
    gk_hbm,
    gv_hbm,
    gg_hbm,
    gg_sum_ref,
    q,
    k,
    v,
    gate,
    go,
    attn,
    dg,
    da,
    gq,
    gk,
    gv,
    gg,
    gk_in,
    gv_in,
    mask,
    mask_t,
    acc_sq,
    acc_cr,
    rb,
    cb,
    st,
    r1,
    tb,
    r2,
    xb,
    r3,
    pb,
    pr,
    prefb,
    sb,
    hr,
    gp,
    gr1,
    gt,
    gr2,
    in_sem,
    kv_sem,
    out_sem,
    s1,
    v1,
    s2,
    v2,
    s3,
    v3,
    s4,
    v4,
    sh,
    vh,
    sg1,
    vg1,
    sg2,
    vg2,
):
    seq = lax.axis_index("seq")
    head = lax.axis_index("head")
    z = seq // NY
    y = lax.rem(seq, NY)
    per = heads // CHUNKS
    crow = per * HD
    prow = crow // NY
    zrow = prow // nz

    def cols(h):
        return pl.ds(pl.multiple_of(h * HD, HD), HD)

    def ypeer(d):
        yp = lax.rem(y + d, NY)
        return yp, (z * NY + yp, head)

    def zpeer(d):
        zp = lax.rem(z + d, nz)
        return zp, (zp * NY + y, head)

    def hpeer(d):
        return (seq, lax.rem(head + d, nh))

    def rcopy(src, dst, ss, rs, dev):
        return pltpu.make_async_remote_copy(
            src_ref=src, dst_ref=dst, send_sem=ss, recv_sem=rs, device_id=dev, device_id_type=MESH
        )

    bar = pltpu.get_barrier_semaphore()

    def greet(dev):
        pl.semaphore_signal(bar, inc=1, device_id=dev, device_id_type=MESH)

    each(1, NY, lambda d: greet(ypeer(d)[1]))
    each(1, nz, lambda d: greet(zpeer(d)[1]))
    each(1, nh, lambda d: greet(hpeer(d)))

    def kv_copy(c, i):
        src, dst = ((k_hbm, k), (v_hbm, v))[i]
        w = pl.ds(c * crow, crow)
        return pltpu.make_async_copy(src.at[:, w], dst.at[:, w], kv_sem.at[c, i])

    for c in range(CHUNKS):
        kv_copy(c, 0).start()
        kv_copy(c, 1).start()
    loads = [
        pltpu.make_async_copy(a, b, in_sem.at[i])
        for i, (a, b) in enumerate(((q_hbm, q), (go_hbm, go), (gate_hbm, gate)))
    ]
    for cp in loads:
        cp.start()

    def p1(s, c, d):
        yp, dev = ypeer(d)
        src = st.at[s, pl.ds(pl.multiple_of(c * crow + yp * prow, 8), prow)]
        return rcopy(src, r1.at[s, c, y], s1.at[s, c, d - 1], v1.at[s, c, d - 1], dev)

    def p2(s, c, d):
        zp, dev = zpeer(d)
        src = tb.at[s, c, pl.ds(pl.multiple_of(zp * zrow, 8), zrow)]
        return rcopy(src, r2.at[s, c, z], s2.at[s, c, d - 1], v2.at[s, c, d - 1], dev)

    def p3(s, c, d):
        zp, dev = zpeer(d)
        dst = r3.at[s, c, pl.ds(pl.multiple_of(z * zrow, 8), zrow)]
        return rcopy(xb.at[s, c, zp], dst, s3.at[s, c, d - 1], v3.at[s, c, d - 1], dev)

    def p4(s, c, d):
        yp, dev = ypeer(d)
        dst = pr.at[s, pl.ds(pl.multiple_of(c * crow + y * prow, 8), prow)]
        return rcopy(pb.at[s, c, yp], dst, s4.at[s, c, d - 1], v4.at[s, c, d - 1], dev)

    def start_p1(s, c):
        own = st[s, pl.ds(pl.multiple_of(c * crow + y * prow, 8), prow)]
        each(1, NY, lambda d: p1(s, c, d).start())
        r1[s, c, y] = own

    def step_a(s, c):
        each(1, NY, lambda d: p1(s, c, d).wait_recv())
        t = r1[s, c, 0]
        for i in range(1, NY):
            t = t + r1[s, c, i]
        tb[s, c] = t
        each(1, nz, lambda d: p2(s, c, d).start())
        r2[s, c, z] = tb[s, c, pl.ds(pl.multiple_of(z * zrow, 8), zrow)]

    def step_b(s, c):
        each(1, nz, lambda d: p2(s, c, d).wait_recv())
        x = jnp.zeros((zrow, HD), F32)
        for i in range(nz) if s == 0 else reversed(range(nz)):
            xb[s, c, i] = x
            x = x + r2[s, c, i]
        each(1, nz, lambda d: p3(s, c, d).start())
        r3[s, c, pl.ds(pl.multiple_of(z * zrow, 8), zrow)] = xb[s, c, z]

    def step_c(s, c):
        each(1, nz, lambda d: p3(s, c, d).wait_recv())
        x = r3[s, c]
        for i in range(NY) if s == 0 else reversed(range(NY)):
            pb[s, c, i] = x
            x = x + r1[s, c, i]
        each(1, NY, lambda d: p4(s, c, d).start())
        pr[s, pl.ds(pl.multiple_of(c * crow + y * prow, 8), prow)] = pb[s, c, y]

    def wait_d(s, c):
        each(1, NY, lambda d: p4(s, c, d).wait_recv())

    def wait_sends(s):
        def one(c):
            each(1, NY, lambda d: p1(s, c, d).wait_send())
            each(1, nz, lambda d: p2(s, c, d).wait_send())
            each(1, nz, lambda d: p3(s, c, d).wait_send())
            each(1, NY, lambda d: p4(s, c, d).wait_send())

        each(0, CHUNKS, one)

    def state(c):
        def one(h):
            w = cols(h)
            st[0, pl.ds(pl.multiple_of(h * HD, HD), HD)] = dot_tn(k[:, w], v[:, w])

        each(c * per, (c + 1) * per, one)

    for c in range(CHUNKS):
        kv_copy(c, 0).wait()
        kv_copy(c, 1).wait()
        state(c)
        if c == 0:
            pl.semaphore_wait(bar, NY + nz + nh - 3)
        start_p1(0, c)

    tiles = rows // TILE
    at_row = lax.broadcasted_iota(jnp.int32, (TILE, TILE), 0)
    at_col = lax.broadcasted_iota(jnp.int32, (TILE, TILE), 1)
    for i in range(tiles):
        for j in range(tiles):
            on = jnp.full((TILE, TILE), tm_ref[i, j], jnp.int32) == 1
            low = on & (at_row >= at_col) if i == j else on
            high = on & (at_col >= at_row) if i == j else on
            ri, cj = pl.ds(i * TILE, TILE), pl.ds(j * TILE, TILE)
            mask[ri, cj] = jnp.where(low, 1.0, 0.0).astype(BF)
            mask_t[cj, ri] = jnp.where(high, 1.0, 0.0).astype(BF)

    for cp in loads:
        cp.wait()

    half = rows // 2
    lower = ((0, half, half), (half, half, rows))
    upper = ((0, half, 0, rows), (half, half, half, half))

    def fwd(h):
        w = cols(h)
        for r0, rn, cn in lower:
            sc = dot_nt(q[r0 : r0 + rn, w], k[0:cn, w])
            p = sc.astype(BF) * mask[r0 : r0 + rn, 0:cn]
            attn[r0 : r0 + rn, w] = dot(p, v[0:cn, w])
        sig = jax.nn.sigmoid(gate[:, w].astype(F32))
        dg[:, w] = go[:, w].astype(F32) * sig * gain_ref[:, w]

    def finish_attn(h):
        w = cols(h)
        pf = pr[0, pl.ds(pl.multiple_of(h * HD, HD), HD)].astype(BF)
        prefb[h] = pf
        a = attn[:, w] + dot(q[:, w], pf)
        attn[:, w] = a
        acc_sq[...] += a * a
        acc_cr[...] += dg[:, w] * a

    acc_sq[...] = jnp.zeros_like(acc_sq)
    acc_cr[...] = jnp.zeros_like(acc_cr)

    def scan1(i):
        @pl.when(i < heads)
        def _():
            fwd(i)

        @pl.when((i >= 2) & (i < 2 + CHUNKS))
        def _():
            step_a(0, i - 2)

        @pl.when((i >= 5) & (i < 5 + CHUNKS))
        def _():
            step_b(0, i - 5)

        @pl.when((i >= 8) & (i < 8 + CHUNKS))
        def _():
            step_c(0, i - 8)

        @pl.when(i >= 12)
        def _():
            c = i - 12
            wait_d(0, c)
            each(c * per, (c + 1) * per, finish_attn)

    each(0, 12 + CHUNKS, scan1)

    sq_t = jnp.sum(acc_sq[...].T, axis=0, keepdims=True)
    cr_t = jnp.sum(acc_cr[...].T, axis=0, keepdims=True)
    for i in range(tiles):
        sb[i : i + 1] = sq_t[:, i * TILE : (i + 1) * TILE]
        sb[tiles + i : tiles + i + 1] = cr_t[:, i * TILE : (i + 1) * TILE]

    def hx(d):
        return rcopy(sb, hr.at[head], sh.at[d - 1], vh.at[d - 1], hpeer(d))

    each(1, nh, lambda d: hx(d).start())
    hr[head] = sb[...]
    each(1, nh, lambda d: hx(d).wait_recv())
    tot = hr[0]
    for i in range(1, nh):
        tot = tot + hr[i]
    ms = tot[0:tiles] * (1.0 / full) + 1e-06
    inv = 1.0 / jnp.sqrt(ms)
    cross = tot[tiles : 2 * tiles] * (1.0 / full) / ms * inv
    for i in range(tiles):
        rb[i * TILE : (i + 1) * TILE] = jnp.broadcast_to(inv[i : i + 1], (TILE, TILE)).T
        cb[i * TILE : (i + 1) * TILE] = jnp.broadcast_to(cross[i : i + 1], (TILE, TILE)).T

    def adjoint(h):
        w = cols(h)
        d = (dg[:, w] * rb[...] - attn[:, w] * cb[...]).astype(BF)
        da[:, w] = d
        st[1, pl.ds(pl.multiple_of(h * HD, HD), HD)] = dot_tn(q[:, w], d)

    def adj_chunk(c):
        each(c * per, (c + 1) * per, adjoint)
        start_p1(1, c)

    each(0, CHUNKS, adj_chunk)

    def gates(h):
        w = cols(h)
        sig = jax.nn.sigmoid(gate[:, w].astype(F32))
        norm = attn[:, w] * rb[...]
        gg[:, w] = (norm * dg[:, w] * (1.0 - sig)).astype(BF)
        gp[pl.ds(h, 1)] = jnp.sum(go[:, w].astype(F32) * sig * norm, axis=0, keepdims=True)

    def bwd(h):
        w = cols(h)
        pf = prefb[h]
        for r0, rn, cn in lower:
            d = da[r0 : r0 + rn, w]
            dp = dot_nt(d, v[0:cn, w]).astype(BF) * mask[r0 : r0 + rn, 0:cn]
            gq[r0 : r0 + rn, w] = (dot(dp, k[0:cn, w]) + dot_nt(d, pf)).astype(BF)
        for r0, rn, c0, cn in upper:
            d = da[c0 : c0 + cn, w]
            qq = q[c0 : c0 + cn, w]
            m = mask_t[r0 : r0 + rn, c0 : c0 + cn]
            dp = dot_nt(v[r0 : r0 + rn, w], d).astype(BF) * m
            gk_in[r0 : r0 + rn, w] = dot(dp, qq)
            pp = dot_nt(k[r0 : r0 + rn, w], qq).astype(BF) * m
            gv_in[r0 : r0 + rn, w] = dot(pp, d)

    def finish(h):
        w = cols(h)
        sf = pr[1, pl.ds(pl.multiple_of(h * HD, HD), HD)].astype(BF)
        gk[:, w] = (gk_in[:, w] + dot_nt(v[:, w], sf)).astype(BF)
        gv[:, w] = (gv_in[:, w] + dot(k[:, w], sf)).astype(BF)

    def gx1(d):
        return rcopy(gp, gr1.at[y], sg1.at[d - 1], vg1.at[d - 1], ypeer(d)[1])

    def gx2(d):
        return rcopy(gt, gr2.at[z], sg2.at[d - 1], vg2.at[d - 1], zpeer(d)[1])

    outs = ((gq, gq_hbm), (gg, gg_hbm), (gk, gk_hbm), (gv, gv_hbm))

    def out_copy(i, c):
        w = pl.ds(pl.multiple_of(c * crow, crow), crow)
        return pltpu.make_async_copy(outs[i][0].at[:, w], outs[i][1].at[:, w], out_sem.at[i, c])

    def scan2(i):
        @pl.when(i < 4)
        def _():
            each(i * per, (i + 1) * per, gates)
            out_copy(1, i).start()

        @pl.when(i == 3)
        def _():
            each(1, NY, lambda d: gx1(d).start())
            gr1[y] = gp[...]

        @pl.when(i < heads)
        def _():
            bwd(i)

        @pl.when((i < heads) & (lax.rem(i, per) == per - 1))
        def _():
            out_copy(0, i // per).start()

        @pl.when((i >= 1) & (i < 1 + CHUNKS))
        def _():
            step_a(1, i - 1)

        @pl.when((i >= 4) & (i < 4 + CHUNKS))
        def _():
            step_b(1, i - 4)

        @pl.when(i == 6)
        def _():
            each(1, NY, lambda d: gx1(d).wait_recv())
            t = gr1[0]
            for n in range(1, NY):
                t = t + gr1[n]
            gt[...] = t
            each(1, nz, lambda d: gx2(d).start())
            gr2[z] = t

        @pl.when((i >= 7) & (i < 7 + CHUNKS))
        def _():
            step_c(1, i - 7)

        @pl.when(i >= 11)
        def _():
            c = i - 11
            wait_d(1, c)
            each(c * per, (c + 1) * per, finish)
            out_copy(2, c).start()
            out_copy(3, c).start()

    each(0, 11 + CHUNKS, scan2)

    each(1, nz, lambda d: gx2(d).wait_recv())
    t = gr2[0]
    for n in range(1, nz):
        t = t + gr2[n]
    gg_sum_ref[...] = t

    wait_sends(0)
    wait_sends(1)
    each(1, nh, lambda d: hx(d).wait_send())
    each(1, NY, lambda d: gx1(d).wait_send())
    each(1, nz, lambda d: gx2(d).wait_send())
    for i in range(4):
        for c in range(CHUNKS):
            out_copy(i, c).wait()


def body(nz, nh, queries, keys, values, gate, grad_out, gain, tile_mask):
    rows, width = queries.shape
    heads = width // HD
    full = width * nh
    per = heads // CHUNKS
    crow = per * HD
    prow = crow // NY
    zrow = prow // nz
    dma = pltpu.SemaphoreType.DMA
    vm = pltpu.VMEM
    big = jax.ShapeDtypeStruct((rows, width), BF)
    scratch = (
        [vm((rows, width), BF)] * 5
        + [vm((rows, width), F32)] * 2
        + [vm((rows, width), BF)] * 5
        + [vm((rows, width), F32)] * 2
        + [vm((rows, rows), BF)] * 2
        + [vm((rows, HD), F32)] * 4
        + [
            vm((2, heads * HD, HD), F32),
            vm((2, CHUNKS, NY, prow, HD), F32),
            vm((2, CHUNKS, prow, HD), F32),
            vm((2, CHUNKS, nz, zrow, HD), F32),
            vm((2, CHUNKS, nz, zrow, HD), F32),
            vm((2, CHUNKS, prow, HD), F32),
            vm((2, CHUNKS, NY, prow, HD), F32),
            vm((2, heads * HD, HD), F32),
            vm((heads, HD, HD), BF),
            vm((8, HD), F32),
            vm((nh, 8, HD), F32),
            vm((heads, HD), F32),
            vm((NY, heads, HD), F32),
            vm((heads, HD), F32),
            vm((nz, heads, HD), F32),
            dma((3,)),
            dma((CHUNKS, 2)),
            dma((4, CHUNKS)),
            dma((2, CHUNKS, NY - 1)),
            dma((2, CHUNKS, NY - 1)),
            dma((2, CHUNKS, nz - 1)),
            dma((2, CHUNKS, nz - 1)),
            dma((2, CHUNKS, nz - 1)),
            dma((2, CHUNKS, nz - 1)),
            dma((2, CHUNKS, NY - 1)),
            dma((2, CHUNKS, NY - 1)),
            dma((nh - 1,)),
            dma((nh - 1,)),
            dma((NY - 1,)),
            dma((NY - 1,)),
            dma((nz - 1,)),
            dma((nz - 1,)),
        ]
    )
    hbm = pl.BlockSpec(memory_space=pl.ANY)
    out = pl.pallas_call(
        functools.partial(layer_kernel, nz, nh, heads, rows, full),
        out_shape=(big, big, big, big, jax.ShapeDtypeStruct((heads, HD), F32)),
        in_specs=[hbm] * 5
        + [pl.BlockSpec(memory_space=pltpu.VMEM), pl.BlockSpec(memory_space=pltpu.SMEM)],
        out_specs=(hbm, hbm, hbm, hbm, pl.BlockSpec(memory_space=pltpu.VMEM)),
        scratch_shapes=scratch,
        compiler_params=pltpu.CompilerParams(
            collective_id=0, has_side_effects=True, vmem_limit_bytes=60 * 1024 * 1024
        ),
        name="layer",
    )(queries, keys, values, gate, grad_out, gain.reshape(1, width), tile_mask)
    return out[0], out[1], out[2], out[3], out[4].reshape(width)


def solution(mesh):
    nz = mesh.shape["seq"] // NY
    nh = mesh.shape["head"]
    wide = P("seq", "head")
    return jax.shard_map(
        functools.partial(body, nz, nh),
        mesh=mesh,
        in_specs=(wide, wide, wide, wide, wide, P("head"), P("seq", None)),
        out_specs=(wide, wide, wide, wide, P("head")),
        check_vma=False,
    )
```

```python
import functools

import jax
import jax.numpy as jnp
from jax import lax
from jax.experimental import pallas as pl
from jax.experimental.pallas import tpu as pltpu
from jax.sharding import PartitionSpec as P

HD = 128
TILE = 128
NY = 4
CHUNKS = 4
MESH = pl.DeviceIdType.MESH
F32 = jnp.float32
BF = jnp.bfloat16


def dot(a, b):
    return lax.dot_general(a, b, (((1,), (0,)), ((), ())), preferred_element_type=F32)


def dot_nt(a, b):
    return lax.dot_general(a, b, (((1,), (1,)), ((), ())), preferred_element_type=F32)


def dot_tn(a, b):
    return lax.dot_general(a, b, (((0,), (0,)), ((), ())), preferred_element_type=F32)


def each(lo, hi, fn):
    def step(i, carry):
        fn(i)
        return carry

    lax.fori_loop(lo, hi, step, 0)


def store_kernel(*refs):
    sem = refs[10]
    copies = [pltpu.make_async_copy(refs[i], refs[5 + i], sem.at[i]) for i in range(5)]
    for cp in copies:
        cp.start()
    for cp in copies:
        cp.wait()


def layer_kernel(
    nz,
    nh,
    heads,
    rows,
    full,
    q_hbm,
    k_hbm,
    v_hbm,
    gate_hbm,
    go_hbm,
    gain_hbm,
    tm_hbm,
    gq,
    gk,
    gv,
    gg,
    gg_sum_ref,
    q,
    k,
    v,
    gate,
    go,
    attn,
    dg,
    da,
    gk_in,
    gv_in,
    mask,
    mask_t,
    acc_sq,
    acc_cr,
    rb,
    cb,
    st,
    r1,
    tb,
    r2,
    xb,
    r3,
    pb,
    pr,
    prefb,
    sb,
    hr,
    gp,
    gr1,
    gt,
    gr2,
    gain_ref,
    tm_ref,
    in_sem,
    kv_sem,
    sent,
    came,
    x_sent,
    x_came,
):
    seq = lax.axis_index("seq")
    head = lax.axis_index("head")
    z = seq // NY
    y = lax.rem(seq, NY)
    per = heads // CHUNKS
    crow = per * HD
    prow = crow // NY
    zrow = prow // nz

    def cols(h):
        return pl.ds(pl.multiple_of(h * HD, HD), HD)

    def ypeer(d):
        yp = lax.rem(y + d, NY)
        return yp, (z * NY + yp, head)

    def zpeer(d):
        zp = lax.rem(z + d, nz)
        return zp, (zp * NY + y, head)

    def hpeer(d):
        return (seq, lax.rem(head + d, nh))

    def rcopy(src, dst, ss, rs, dev):
        return pltpu.make_async_remote_copy(
            src_ref=src, dst_ref=dst, send_sem=ss, recv_sem=rs, device_id=dev, device_id_type=MESH
        )

    bar = pltpu.get_barrier_semaphore()

    def greet(dev):
        pl.semaphore_signal(bar, inc=1, device_id=dev, device_id_type=MESH)

    each(1, NY, lambda d: greet(ypeer(d)[1]))
    each(1, nz, lambda d: greet(zpeer(d)[1]))
    each(1, nh, lambda d: greet(hpeer(d)))

    def kv_copy(c, i):
        src, dst = ((k_hbm, k), (v_hbm, v))[i]
        w = pl.ds(c * crow, crow)
        return pltpu.make_async_copy(src.at[:, w], dst.at[:, w], kv_sem.at[c, i])

    for c in range(CHUNKS):
        kv_copy(c, 0).start()
        kv_copy(c, 1).start()
    pairs = ((tm_hbm, tm_ref), (gain_hbm, gain_ref), (q_hbm, q), (go_hbm, go), (gate_hbm, gate))
    loads = [
        pltpu.make_async_copy(a, b, in_sem.at[i])
        for i, (a, b) in enumerate(pairs)
    ]
    for cp in loads:
        cp.start()

    def settle(ref, sem):
        pltpu.make_async_copy(ref, ref, sem).wait()

    def p1(s, c, d):
        yp, dev = ypeer(d)
        src = st.at[s, pl.ds(pl.multiple_of(c * crow + yp * prow, 8), prow)]
        return rcopy(src, r1.at[s, c, y], sent.at[s, 0], came.at[s, 0, c], dev)

    def p2(s, c, d):
        zp, dev = zpeer(d)
        src = tb.at[s, c, pl.ds(pl.multiple_of(zp * zrow, 8), zrow)]
        return rcopy(src, r2.at[s, c, z], sent.at[s, 1], came.at[s, 1, c], dev)

    def p3(s, c, d):
        zp, dev = zpeer(d)
        dst = r3.at[s, c, pl.ds(pl.multiple_of(z * zrow, 8), zrow)]
        return rcopy(xb.at[s, c, zp], dst, sent.at[s, 2], came.at[s, 2, c], dev)

    def p4(s, c, d):
        yp, dev = ypeer(d)
        dst = pr.at[s, pl.ds(pl.multiple_of(c * crow + y * prow, 8), prow)]
        return rcopy(pb.at[s, c, yp], dst, sent.at[s, 3], came.at[s, 3, c], dev)

    def start_p1(s, c):
        own = st[s, pl.ds(pl.multiple_of(c * crow + y * prow, 8), prow)]
        each(1, NY, lambda d: p1(s, c, d).start())
        r1[s, c, y] = own

    def step_a(s, c):
        settle(r1.at[s, c, 0 : NY - 1], came.at[s, 0, c])
        t = r1[s, c, 0]
        for i in range(1, NY):
            t = t + r1[s, c, i]
        tb[s, c] = t
        each(1, nz, lambda d: p2(s, c, d).start())
        r2[s, c, z] = tb[s, c, pl.ds(pl.multiple_of(z * zrow, 8), zrow)]

    def step_b(s, c):
        settle(r2.at[s, c, 0 : nz - 1], came.at[s, 1, c])
        x = jnp.zeros((zrow, HD), F32)
        for i in range(nz) if s == 0 else reversed(range(nz)):
            xb[s, c, i] = x
            x = x + r2[s, c, i]
        each(1, nz, lambda d: p3(s, c, d).start())
        r3[s, c, pl.ds(pl.multiple_of(z * zrow, 8), zrow)] = xb[s, c, z]

    def step_c(s, c):
        settle(r3.at[s, c, 0 : (nz - 1) * zrow], came.at[s, 2, c])
        x = r3[s, c]
        for i in range(NY) if s == 0 else reversed(range(NY)):
            pb[s, c, i] = x
            x = x + r1[s, c, i]
        each(1, NY, lambda d: p4(s, c, d).start())
        pr[s, pl.ds(pl.multiple_of(c * crow + y * prow, 8), prow)] = pb[s, c, y]

    def wait_d(s, c):
        settle(pr.at[s, 0 : (NY - 1) * prow], came.at[s, 3, c])

    def wait_sends(s):
        settle(st.at[s, 0 : CHUNKS * (NY - 1) * prow], sent.at[s, 0])
        settle(r2.at[s, :, 0 : nz - 1], sent.at[s, 1])
        settle(xb.at[s, :, 0 : nz - 1], sent.at[s, 2])
        settle(pb.at[s, :, 0 : NY - 1], sent.at[s, 3])

    def state(c):
        def one(h):
            w = cols(h)
            st[0, pl.ds(pl.multiple_of(h * HD, HD), HD)] = dot_tn(k[:, w], v[:, w])

        each(c * per, (c + 1) * per, one)

    for c in range(CHUNKS):
        kv_copy(c, 0).wait()
        kv_copy(c, 1).wait()
        state(c)

    loads[0].wait()
    tiles = rows // TILE
    at_row = lax.broadcasted_iota(jnp.int32, (TILE, TILE), 0)
    at_col = lax.broadcasted_iota(jnp.int32, (TILE, TILE), 1)
    for i in range(tiles):
        for j in range(tiles):
            on = jnp.broadcast_to(tm_ref[i : i + 1, j : j + 1], (TILE, TILE)) == 1
            low = on & (at_row >= at_col) if i == j else on
            high = on & (at_col >= at_row) if i == j else on
            ri, cj = pl.ds(i * TILE, TILE), pl.ds(j * TILE, TILE)
            mask[ri, cj] = jnp.where(low, 1.0, 0.0).astype(BF)
            mask_t[cj, ri] = jnp.where(high, 1.0, 0.0).astype(BF)

    pl.semaphore_wait(bar, NY + nz + nh - 3)
    each(0, CHUNKS, lambda c: start_p1(0, c))

    for cp in loads[1:]:
        cp.wait()

    half = rows // 2
    lower = ((0, half, half), (half, half, rows))
    upper = ((0, half, 0, rows), (half, half, half, half))

    def fwd(h):
        w = cols(h)
        for r0, rn, cn in lower:
            sc = dot_nt(q[r0 : r0 + rn, w], k[0:cn, w])
            p = sc.astype(BF) * mask[r0 : r0 + rn, 0:cn]
            attn[r0 : r0 + rn, w] = dot(p, v[0:cn, w])
        sig = jax.nn.sigmoid(gate[:, w].astype(F32))
        dg[:, w] = go[:, w].astype(F32) * sig * gain_ref[:, w]

    def finish_attn(h):
        w = cols(h)
        pf = pr[0, pl.ds(pl.multiple_of(h * HD, HD), HD)].astype(BF)
        prefb[h] = pf
        a = attn[:, w] + dot(q[:, w], pf)
        attn[:, w] = a
        acc_sq[...] += a * a
        acc_cr[...] += dg[:, w] * a

    acc_sq[...] = jnp.zeros_like(acc_sq)
    acc_cr[...] = jnp.zeros_like(acc_cr)

    def scan1(i):
        @pl.when(i < heads)
        def _():
            fwd(i)

        @pl.when((i >= 2) & (i < 2 + CHUNKS))
        def _():
            step_a(0, i - 2)

        @pl.when((i >= 5) & (i < 5 + CHUNKS))
        def _():
            step_b(0, i - 5)

        @pl.when((i >= 8) & (i < 8 + CHUNKS))
        def _():
            step_c(0, i - 8)

        @pl.when(i >= 12)
        def _():
            c = i - 12
            wait_d(0, c)
            each(c * per, (c + 1) * per, finish_attn)

    each(0, 12 + CHUNKS, scan1)

    eye = jnp.where(at_row == at_col, 1.0, 0.0)
    for i in range(tiles):
        ri = slice(i * TILE, (i + 1) * TILE)
        for n, acc in ((i, acc_sq), (tiles + i, acc_cr)):
            total = jnp.sum(acc[ri], axis=1, keepdims=True)
            sb[n : n + 1] = jnp.sum(total * eye, axis=0, keepdims=True)

    def hx(d):
        return rcopy(sb, hr.at[head], x_sent.at[0], x_came.at[0], hpeer(d))

    each(1, nh, lambda d: hx(d).start())
    hr[head] = sb[...]
    settle(hr.at[0 : nh - 1], x_came.at[0])
    tot = hr[0]
    for i in range(1, nh):
        tot = tot + hr[i]
    ms = tot[0:tiles] * (1.0 / full) + 1e-06
    inv = 1.0 / jnp.sqrt(ms)
    cross = tot[tiles : 2 * tiles] * (1.0 / full) / ms * inv
    for i in range(tiles):
        ri = slice(i * TILE, (i + 1) * TILE)
        for line, wide in ((inv, rb), (cross, cb)):
            col = jnp.sum(line[i : i + 1] * eye, axis=1, keepdims=True)
            wide[ri] = jnp.broadcast_to(col, (TILE, HD))

    def adjoint(h):
        w = cols(h)
        d = (dg[:, w] * rb[...] - attn[:, w] * cb[...]).astype(BF)
        da[:, w] = d
        st[1, pl.ds(pl.multiple_of(h * HD, HD), HD)] = dot_tn(q[:, w], d)

    def adj_chunk(c):
        each(c * per, (c + 1) * per, adjoint)
        start_p1(1, c)

    each(0, CHUNKS, adj_chunk)

    def gates(h):
        w = cols(h)
        sig = jax.nn.sigmoid(gate[:, w].astype(F32))
        norm = attn[:, w] * rb[...]
        gg[:, w] = (norm * dg[:, w] * (1.0 - sig)).astype(BF)
        gp[pl.ds(h, 1)] = jnp.sum(go[:, w].astype(F32) * sig * norm, axis=0, keepdims=True)

    def bwd(h):
        w = cols(h)
        pf = prefb[h]
        for r0, rn, cn in lower:
            d = da[r0 : r0 + rn, w]
            dp = dot_nt(d, v[0:cn, w]).astype(BF) * mask[r0 : r0 + rn, 0:cn]
            gq[r0 : r0 + rn, w] = (dot(dp, k[0:cn, w]) + dot_nt(d, pf)).astype(BF)
        for r0, rn, c0, cn in upper:
            d = da[c0 : c0 + cn, w]
            qq = q[c0 : c0 + cn, w]
            m = mask_t[r0 : r0 + rn, c0 : c0 + cn]
            dp = dot_nt(v[r0 : r0 + rn, w], d).astype(BF) * m
            gk_in[r0 : r0 + rn, w] = dot(dp, qq)
            pp = dot_nt(k[r0 : r0 + rn, w], qq).astype(BF) * m
            gv_in[r0 : r0 + rn, w] = dot(pp, d)

    def finish(h):
        w = cols(h)
        sf = pr[1, pl.ds(pl.multiple_of(h * HD, HD), HD)].astype(BF)
        gk[:, w] = (gk_in[:, w] + dot_nt(v[:, w], sf)).astype(BF)
        gv[:, w] = (gv_in[:, w] + dot(k[:, w], sf)).astype(BF)

    def gx1(d):
        return rcopy(gp, gr1.at[y], x_sent.at[1], x_came.at[1], ypeer(d)[1])

    def gx2(d):
        return rcopy(gt, gr2.at[z], x_sent.at[2], x_came.at[2], zpeer(d)[1])

    def scan2(i):
        @pl.when(i < 4)
        def _():
            each(i * per, (i + 1) * per, gates)

        @pl.when(i == 3)
        def _():
            each(1, NY, lambda d: gx1(d).start())
            gr1[y] = gp[...]

        @pl.when(i < heads)
        def _():
            bwd(i)

        @pl.when((i >= 1) & (i < 1 + CHUNKS))
        def _():
            step_a(1, i - 1)

        @pl.when((i >= 4) & (i < 4 + CHUNKS))
        def _():
            step_b(1, i - 4)

        @pl.when(i == 6)
        def _():
            settle(gr1.at[0 : NY - 1], x_came.at[1])
            t = gr1[0]
            for n in range(1, NY):
                t = t + gr1[n]
            gt[...] = t
            each(1, nz, lambda d: gx2(d).start())
            gr2[z] = t

        @pl.when((i >= 7) & (i < 7 + CHUNKS))
        def _():
            step_c(1, i - 7)

        @pl.when(i >= 11)
        def _():
            c = i - 11
            wait_d(1, c)
            each(c * per, (c + 1) * per, finish)

    each(0, 11 + CHUNKS, scan2)

    settle(gr2.at[0 : nz - 1], x_came.at[2])
    t = gr2[0]
    for n in range(1, nz):
        t = t + gr2[n]
    gg_sum_ref[...] = t

    wait_sends(0)
    wait_sends(1)
    settle(hr.at[0 : nh - 1], x_sent.at[0])
    settle(gr1.at[0 : NY - 1], x_sent.at[1])
    settle(gr2.at[0 : nz - 1], x_sent.at[2])


def body(nz, nh, queries, keys, values, gate, grad_out, gain, tile_mask):
    rows, width = queries.shape
    heads = width // HD
    full = width * nh
    per = heads // CHUNKS
    crow = per * HD
    prow = crow // NY
    zrow = prow // nz
    dma = pltpu.SemaphoreType.DMA
    vm = pltpu.VMEM
    big = jax.ShapeDtypeStruct((rows, width), BF)
    scratch = (
        [vm((rows, width), BF)] * 5
        + [vm((rows, width), F32)] * 2
        + [vm((rows, width), BF)]
        + [vm((rows, width), F32)] * 2
        + [vm((rows, rows), BF)] * 2
        + [vm((rows, HD), F32)] * 4
        + [
            vm((2, heads * HD, HD), F32),
            vm((2, CHUNKS, NY, prow, HD), F32),
            vm((2, CHUNKS, prow, HD), F32),
            vm((2, CHUNKS, nz, zrow, HD), F32),
            vm((2, CHUNKS, nz, zrow, HD), F32),
            vm((2, CHUNKS, prow, HD), F32),
            vm((2, CHUNKS, NY, prow, HD), F32),
            vm((2, heads * HD, HD), F32),
            vm((heads, HD, HD), BF),
            vm((8, HD), F32),
            vm((nh, 8, HD), F32),
            vm((heads, HD), F32),
            vm((NY, heads, HD), F32),
            vm((heads, HD), F32),
            vm((nz, heads, HD), F32),
            vm((1, width), F32),
            vm(tile_mask.shape, jnp.int32),
            dma((5,)),
            dma((CHUNKS, 2)),
            dma((2, 4)),
            dma((2, 4, CHUNKS)),
            dma((3,)),
            dma((3,)),
        ]
    )
    hbm = pl.BlockSpec(memory_space=pl.ANY)
    args = (queries, keys, values, gate, grad_out, gain.reshape(1, width), tile_mask)
    parts = pl.pallas_call(
        functools.partial(layer_kernel, nz, nh, heads, rows, full),
        out_shape=(big, big, big, big, jax.ShapeDtypeStruct((heads, HD), F32)),
        in_specs=[hbm] * 7,
        out_specs=(pl.BlockSpec(memory_space=pltpu.VMEM),) * 5,
        scratch_shapes=scratch,
        compiler_params=pltpu.CompilerParams(
            collective_id=0, has_side_effects=True, vmem_limit_bytes=36 * 1024 * 1024
        ),
        name="layer",
    )(*(pltpu.with_memory_space_constraint(a, pltpu.HBM) for a in args))
    out = pl.pallas_call(
        store_kernel,
        out_shape=(big, big, big, big, jax.ShapeDtypeStruct((heads, HD), F32)),
        in_specs=[pl.BlockSpec(memory_space=pltpu.VMEM)] * 5,
        out_specs=(hbm,) * 5,
        scratch_shapes=[dma((5,))],
        compiler_params=pltpu.CompilerParams(vmem_limit_bytes=8 * 1024 * 1024),
        name="store",
    )(*parts)
    return out[0], out[1], out[2], out[3], out[4].reshape(width)


def solution(mesh):
    nz = mesh.shape["seq"] // NY
    nh = mesh.shape["head"]
    wide = P("seq", "head")
    return jax.shard_map(
        functools.partial(body, nz, nh),
        mesh=mesh,
        in_specs=(wide, wide, wide, wide, wide, P("head"), P("seq", None)),
        out_specs=(wide, wide, wide, wide, P("head")),
        check_vma=False,
    )
```

```python
import functools

import jax
import jax.numpy as jnp
from jax import lax
from jax.experimental import pallas as pl
from jax.experimental.pallas import tpu as pltpu
from jax.sharding import PartitionSpec as P

HD = 128
TILE = 128
NY = 4
CHUNKS = 4
Y_ORDER = (2, 1, 3)
AHEAD = 4
MESH = pl.DeviceIdType.MESH
F32 = jnp.float32
BF = jnp.bfloat16


def dot(a, b):
    return lax.dot_general(a, b, (((1,), (0,)), ((), ())), preferred_element_type=F32)


def dot_nt(a, b):
    return lax.dot_general(a, b, (((1,), (1,)), ((), ())), preferred_element_type=F32)


def dot_tn(a, b):
    return lax.dot_general(a, b, (((0,), (0,)), ((), ())), preferred_element_type=F32)


def each(lo, hi, fn):
    def step(i, carry):
        fn(i)
        return carry

    lax.fori_loop(lo, hi, step, 0)


def far_first(n):
    return sorted(range(1, n), key=lambda d: -min(d, n - d))


def store_kernel(*refs):
    sem = refs[10]
    copies = [pltpu.make_async_copy(refs[i], refs[5 + i], sem.at[i]) for i in range(5)]
    for cp in copies:
        cp.start()
    for cp in copies:
        cp.wait()


def layer_kernel(
    nz,
    nh,
    heads,
    rows,
    full,
    q_hbm,
    k_hbm,
    v_hbm,
    gate_hbm,
    go_hbm,
    gain_hbm,
    tm_hbm,
    gq,
    gk,
    gv,
    gg,
    gg_sum_ref,
    q,
    k,
    v,
    gate,
    go,
    attn,
    dg,
    da,
    gk_in,
    gv_in,
    mask,
    mask_t,
    probs_t,
    dn,
    slope,
    acc_sq,
    acc_cr,
    rb,
    cb,
    st,
    r1,
    tb,
    r2,
    xb,
    r3,
    pb,
    pr,
    prefb,
    sb,
    hr,
    gp,
    gr1,
    gt,
    gr2,
    gain_ref,
    tm_ref,
    in_sem,
    kv_sem,
    sent,
    came,
    x_sent,
    x_came,
):
    seq = lax.axis_index("seq")
    head = lax.axis_index("head")
    z = seq // NY
    y = lax.rem(seq, NY)
    per = heads // CHUNKS
    crow = per * HD
    prow = crow // NY
    zrow = prow // nz

    def cols(h):
        return pl.ds(pl.multiple_of(h * HD, HD), HD)

    def ypeer(d):
        yp = lax.rem(y + d, NY)
        return yp, (z * NY + yp, head)

    def zpeer(d):
        zp = lax.rem(z + d, nz)
        return zp, (zp * NY + y, head)

    def hpeer(d):
        return (seq, lax.rem(head + d, nh))

    def rcopy(src, dst, ss, rs, dev):
        return pltpu.make_async_remote_copy(
            src_ref=src, dst_ref=dst, send_sem=ss, recv_sem=rs, device_id=dev, device_id_type=MESH
        )

    bar = pltpu.get_barrier_semaphore()

    def greet(dev):
        pl.semaphore_signal(bar, inc=1, device_id=dev, device_id_type=MESH)

    each(1, NY, lambda d: greet(ypeer(d)[1]))
    each(1, nz, lambda d: greet(zpeer(d)[1]))
    each(1, nh, lambda d: greet(hpeer(d)))

    def kv_copy(c, i):
        src, dst = ((k_hbm, k), (v_hbm, v))[i]
        w = pl.ds(c * crow, crow)
        return pltpu.make_async_copy(src.at[:, w], dst.at[:, w], kv_sem.at[c, i])

    for c in range(CHUNKS):
        kv_copy(c, 0).start()
        kv_copy(c, 1).start()
    pairs = ((tm_hbm, tm_ref), (gain_hbm, gain_ref), (q_hbm, q), (go_hbm, go), (gate_hbm, gate))
    loads = [
        pltpu.make_async_copy(a, b, in_sem.at[i])
        for i, (a, b) in enumerate(pairs)
    ]
    for cp in loads:
        cp.start()

    def settle(ref, sem):
        pltpu.make_async_copy(ref, ref, sem).wait()

    def p1(s, c, d):
        yp, dev = ypeer(d)
        src = st.at[s, pl.ds(pl.multiple_of(c * crow + yp * prow, 8), prow)]
        return rcopy(src, r1.at[s, c, y], sent.at[s, 0], came.at[s, 0, c], dev)

    def p2(s, c, d):
        zp, dev = zpeer(d)
        src = tb.at[s, c, pl.ds(pl.multiple_of(zp * zrow, 8), zrow)]
        return rcopy(src, r2.at[s, c, z], sent.at[s, 1], came.at[s, 1, c], dev)

    def p3(s, c, d):
        zp, dev = zpeer(d)
        dst = r3.at[s, c, pl.ds(pl.multiple_of(z * zrow, 8), zrow)]
        return rcopy(xb.at[s, c, zp], dst, sent.at[s, 2], came.at[s, 2, c], dev)

    def p4(s, c, d):
        yp, dev = ypeer(d)
        dst = pr.at[s, pl.ds(pl.multiple_of(c * crow + y * prow, 8), prow)]
        return rcopy(pb.at[s, c, yp], dst, sent.at[s, 3], came.at[s, 3, c], dev)

    def start_p1(s, c):
        own = st[s, pl.ds(pl.multiple_of(c * crow + y * prow, 8), prow)]
        for d in Y_ORDER:
            p1(s, c, d).start()
        r1[s, c, y] = own

    def step_a(s, c):
        settle(r1.at[s, c, 0 : NY - 1], came.at[s, 0, c])
        t = r1[s, c, 0]
        for i in range(1, NY):
            t = t + r1[s, c, i]
        tb[s, c] = t
        for d in far_first(nz):
            p2(s, c, d).start()
        r2[s, c, z] = tb[s, c, pl.ds(pl.multiple_of(z * zrow, 8), zrow)]

    def step_b(s, c):
        settle(r2.at[s, c, 0 : nz - 1], came.at[s, 1, c])
        x = jnp.zeros((zrow, HD), F32)
        for i in range(nz) if s == 0 else reversed(range(nz)):
            xb[s, c, i] = x
            x = x + r2[s, c, i]
        for d in far_first(nz):
            p3(s, c, d).start()
        r3[s, c, pl.ds(pl.multiple_of(z * zrow, 8), zrow)] = xb[s, c, z]

    def step_c(s, c):
        settle(r3.at[s, c, 0 : (nz - 1) * zrow], came.at[s, 2, c])
        x = r3[s, c]
        for i in range(NY) if s == 0 else reversed(range(NY)):
            pb[s, c, i] = x
            x = x + r1[s, c, i]
        for d in Y_ORDER:
            p4(s, c, d).start()
        pr[s, pl.ds(pl.multiple_of(c * crow + y * prow, 8), prow)] = pb[s, c, y]

    def wait_d(s, c):
        settle(pr.at[s, 0 : (NY - 1) * prow], came.at[s, 3, c])

    def wait_sends(s):
        settle(st.at[s, 0 : CHUNKS * (NY - 1) * prow], sent.at[s, 0])
        settle(r2.at[s, :, 0 : nz - 1], sent.at[s, 1])
        settle(xb.at[s, :, 0 : nz - 1], sent.at[s, 2])
        settle(pb.at[s, :, 0 : NY - 1], sent.at[s, 3])

    def state(c):
        def one(h):
            w = cols(h)
            st[0, pl.ds(pl.multiple_of(h * HD, HD), HD)] = dot_tn(k[:, w], v[:, w])

        each(c * per, (c + 1) * per, one)

    for c in range(CHUNKS):
        kv_copy(c, 0).wait()
        kv_copy(c, 1).wait()
        state(c)

    loads[0].wait()
    tiles = rows // TILE
    at_row = lax.broadcasted_iota(jnp.int32, (TILE, TILE), 0)
    at_col = lax.broadcasted_iota(jnp.int32, (TILE, TILE), 1)
    for i in range(tiles):
        for j in range(tiles):
            on = jnp.broadcast_to(tm_ref[i : i + 1, j : j + 1], (TILE, TILE)) == 1
            low = on & (at_row >= at_col) if i == j else on
            high = on & (at_col >= at_row) if i == j else on
            ri, cj = pl.ds(i * TILE, TILE), pl.ds(j * TILE, TILE)
            mask[ri, cj] = jnp.where(low, 1.0, 0.0).astype(BF)
            mask_t[cj, ri] = jnp.where(high, 1.0, 0.0).astype(BF)

    pl.semaphore_wait(bar, NY + nz + nh - 3)
    each(0, CHUNKS, lambda c: start_p1(0, c))

    for cp in loads[1:]:
        cp.wait()

    half = rows // 2
    lower = ((0, half, half), (half, half, rows))
    upper = ((0, half, 0, rows), (half, half, half, half))

    def fwd(h):
        w = cols(h)
        for r0, rn, cn in lower:
            sc = dot_nt(q[r0 : r0 + rn, w], k[0:cn, w])
            p = sc.astype(BF) * mask[r0 : r0 + rn, 0:cn]
            attn[r0 : r0 + rn, w] = dot(p, v[0:cn, w])

    def gated(h):
        w = cols(h)
        sig = jax.nn.sigmoid(gate[:, w].astype(F32))
        d = go[:, w].astype(F32) * sig
        g = d * gain_ref[:, w]
        dn[:, w] = d
        dg[:, w] = g
        slope[:, w] = g * (1.0 - sig)

    def turned(h):
        w = cols(h)
        for r0, rn, c0, cn in upper:
            pp = dot_nt(k[r0 : r0 + rn, w], q[c0 : c0 + cn, w]).astype(BF)
            probs_t[h, r0 : r0 + rn, c0 : c0 + cn] = pp * mask_t[r0 : r0 + rn, c0 : c0 + cn]

    def finish_attn(h):
        w = cols(h)
        pf = pr[0, pl.ds(pl.multiple_of(h * HD, HD), HD)].astype(BF)
        prefb[h] = pf
        a = attn[:, w] + dot(q[:, w], pf)
        attn[:, w] = a
        acc_sq[...] += a * a
        acc_cr[...] += dg[:, w] * a

    acc_sq[...] = jnp.zeros_like(acc_sq)
    acc_cr[...] = jnp.zeros_like(acc_cr)

    def during(i, lo, n, fn):
        @pl.when((i >= lo) & (i < lo + n))
        def _():
            fn(i - lo)

    def close1(c):
        wait_d(0, c)
        each(c * per, (c + 1) * per, finish_attn)

    def scan1(i):
        during(i, 0, CHUNKS, lambda c: step_a(0, c))
        during(i, CHUNKS - 1, CHUNKS, lambda c: step_b(0, c))
        during(i, 2 * CHUNKS - 2, CHUNKS, lambda c: step_c(0, c))
        during(i, 0, heads - AHEAD, lambda h: fwd(AHEAD + h))
        during(i, 0, heads, gated)
        during(i, 0, heads, turned)
        during(i, 2 * CHUNKS + 2, CHUNKS, close1)

    each(0, AHEAD, fwd)
    each(0, 3 * CHUNKS + 2, scan1)

    eye = jnp.where(at_row == at_col, 1.0, 0.0)
    for i in range(tiles):
        ri = slice(i * TILE, (i + 1) * TILE)
        for n, acc in ((i, acc_sq), (tiles + i, acc_cr)):
            total = jnp.sum(acc[ri], axis=1, keepdims=True)
            sb[n : n + 1] = jnp.sum(total * eye, axis=0, keepdims=True)

    def hx(d):
        return rcopy(sb, hr.at[head], x_sent.at[0], x_came.at[0], hpeer(d))

    for d in far_first(nh):
        hx(d).start()
    hr[head] = sb[...]
    settle(hr.at[0 : nh - 1], x_came.at[0])
    tot = hr[0]
    for i in range(1, nh):
        tot = tot + hr[i]
    ms = tot[0:tiles] * (1.0 / full) + 1e-06
    inv = 1.0 / jnp.sqrt(ms)
    cross = tot[tiles : 2 * tiles] * (1.0 / full) / ms * inv
    for i in range(tiles):
        ri = slice(i * TILE, (i + 1) * TILE)
        for line, wide in ((inv, rb), (cross, cb)):
            col = jnp.sum(line[i : i + 1] * eye, axis=1, keepdims=True)
            wide[ri] = jnp.broadcast_to(col, (TILE, HD))

    def adjoint(h):
        w = cols(h)
        d = (dg[:, w] * rb[...] - attn[:, w] * cb[...]).astype(BF)
        da[:, w] = d
        st[1, pl.ds(pl.multiple_of(h * HD, HD), HD)] = dot_tn(q[:, w], d)

    def adj_chunk(c):
        each(c * per, (c + 1) * per, adjoint)
        start_p1(1, c)

    each(0, CHUNKS, adj_chunk)

    def gates(h):
        w = cols(h)
        norm = attn[:, w] * rb[...]
        gg[:, w] = (norm * slope[:, w]).astype(BF)
        gp[pl.ds(h, 1)] = jnp.sum(dn[:, w] * norm, axis=0, keepdims=True)

    def bwd(h):
        w = cols(h)
        for r0, rn, cn in lower:
            d = da[r0 : r0 + rn, w]
            dp = dot_nt(d, v[0:cn, w]).astype(BF) * mask[r0 : r0 + rn, 0:cn]
            gq[r0 : r0 + rn, w] = (dot(dp, k[0:cn, w]) + dot_nt(d, prefb[h])).astype(BF)
        for r0, rn, c0, cn in upper:
            d = da[c0 : c0 + cn, w]
            m = mask_t[r0 : r0 + rn, c0 : c0 + cn]
            dp = dot_nt(v[r0 : r0 + rn, w], d).astype(BF) * m
            gk_in[r0 : r0 + rn, w] = dot(dp, q[c0 : c0 + cn, w])
            gv_in[r0 : r0 + rn, w] = dot(probs_t[h, r0 : r0 + rn, c0 : c0 + cn], d)

    def finish(h):
        w = cols(h)
        sf = pr[1, pl.ds(pl.multiple_of(h * HD, HD), HD)].astype(BF)
        gk[:, w] = (gk_in[:, w] + dot_nt(v[:, w], sf)).astype(BF)
        gv[:, w] = (gv_in[:, w] + dot(k[:, w], sf)).astype(BF)

    def gx1(d):
        return rcopy(gp, gr1.at[y], x_sent.at[1], x_came.at[1], ypeer(d)[1])

    def gx2(d):
        return rcopy(gt, gr2.at[z], x_sent.at[2], x_came.at[2], zpeer(d)[1])

    def close2(c):
        wait_d(1, c)
        each(c * per, (c + 1) * per, finish)

    def scan2(i):
        during(i, 0, CHUNKS, lambda c: step_a(1, c))
        during(i, CHUNKS - 1, CHUNKS, lambda c: step_b(1, c))
        during(i, 2 * CHUNKS - 2, CHUNKS, lambda c: step_c(1, c))

        @pl.when(i == CHUNKS - 1)
        def _():
            each(heads // 2, heads, gates)
            each(1, NY, lambda d: gx1(d).start())
            gr1[y] = gp[...]

        @pl.when(i == 2 * CHUNKS)
        def _():
            settle(gr1.at[0 : NY - 1], x_came.at[1])
            t = gr1[0]
            for n in range(1, NY):
                t = t + gr1[n]
            gt[...] = t
            each(1, nz, lambda d: gx2(d).start())
            gr2[z] = t

        @pl.when((i < heads) & (i != CHUNKS - 1))
        def _():
            bwd(jnp.where(i < CHUNKS - 1, i + 1, i))

        during(i, 2 * CHUNKS + 2, CHUNKS, close2)

    each(0, heads // 2, gates)
    bwd(0)
    each(0, 3 * CHUNKS + 2, scan2)

    settle(gr2.at[0 : nz - 1], x_came.at[2])
    t = gr2[0]
    for n in range(1, nz):
        t = t + gr2[n]
    gg_sum_ref[...] = t

    wait_sends(0)
    wait_sends(1)
    settle(hr.at[0 : nh - 1], x_sent.at[0])
    settle(gr1.at[0 : NY - 1], x_sent.at[1])
    settle(gr2.at[0 : nz - 1], x_sent.at[2])


def body(nz, nh, queries, keys, values, gate, grad_out, gain, tile_mask):
    rows, width = queries.shape
    heads = width // HD
    full = width * nh
    per = heads // CHUNKS
    crow = per * HD
    prow = crow // NY
    zrow = prow // nz
    dma = pltpu.SemaphoreType.DMA
    vm = pltpu.VMEM
    big = jax.ShapeDtypeStruct((rows, width), BF)
    scratch = (
        [vm((rows, width), BF)] * 5
        + [vm((rows, width), F32)] * 2
        + [vm((rows, width), BF)]
        + [vm((rows, width), F32)] * 2
        + [vm((rows, rows), BF)] * 2
        + [vm((heads, rows, rows), BF)]
        + [vm((rows, width), F32)] * 2
        + [vm((rows, HD), F32)] * 4
        + [
            vm((2, heads * HD, HD), F32),
            vm((2, CHUNKS, NY, prow, HD), F32),
            vm((2, CHUNKS, prow, HD), F32),
            vm((2, CHUNKS, nz, zrow, HD), F32),
            vm((2, CHUNKS, nz, zrow, HD), F32),
            vm((2, CHUNKS, prow, HD), F32),
            vm((2, CHUNKS, NY, prow, HD), F32),
            vm((2, heads * HD, HD), F32),
            vm((heads, HD, HD), BF),
            vm((8, HD), F32),
            vm((nh, 8, HD), F32),
            vm((heads, HD), F32),
            vm((NY, heads, HD), F32),
            vm((heads, HD), F32),
            vm((nz, heads, HD), F32),
            vm((1, width), F32),
            vm(tile_mask.shape, jnp.int32),
            dma((5,)),
            dma((CHUNKS, 2)),
            dma((2, 4)),
            dma((2, 4, CHUNKS)),
            dma((3,)),
            dma((3,)),
        ]
    )
    hbm = pl.BlockSpec(memory_space=pl.ANY)
    args = (queries, keys, values, gate, grad_out, gain.reshape(1, width), tile_mask)
    parts = pl.pallas_call(
        functools.partial(layer_kernel, nz, nh, heads, rows, full),
        out_shape=(big, big, big, big, jax.ShapeDtypeStruct((heads, HD), F32)),
        in_specs=[hbm] * 7,
        out_specs=(pl.BlockSpec(memory_space=pltpu.VMEM),) * 5,
        scratch_shapes=scratch,
        compiler_params=pltpu.CompilerParams(
            collective_id=0, has_side_effects=True, vmem_limit_bytes=44 * 1024 * 1024
        ),
        name="layer",
    )(*(pltpu.with_memory_space_constraint(a, pltpu.HBM) for a in args))
    out = pl.pallas_call(
        store_kernel,
        out_shape=(big, big, big, big, jax.ShapeDtypeStruct((heads, HD), F32)),
        in_specs=[pl.BlockSpec(memory_space=pltpu.VMEM)] * 5,
        out_specs=(hbm,) * 5,
        scratch_shapes=[dma((5,))],
        compiler_params=pltpu.CompilerParams(vmem_limit_bytes=8 * 1024 * 1024),
        name="store",
    )(*parts)
    return out[0], out[1], out[2], out[3], out[4].reshape(width)


def solution(mesh):
    nz = mesh.shape["seq"] // NY
    nh = mesh.shape["head"]
    wide = P("seq", "head")
    return jax.shard_map(
        functools.partial(body, nz, nh),
        mesh=mesh,
        in_specs=(wide, wide, wide, wide, wide, P("head"), P("seq", None)),
        out_specs=(wide, wide, wide, wide, P("head")),
        check_vma=False,
    )
```

```python
import functools

import jax
import jax.numpy as jnp
from jax import lax
from jax.experimental import pallas as pl
from jax.experimental.pallas import tpu as pltpu
from jax.sharding import PartitionSpec as P

HD = 128
TILE = 128
NY = 4
CHUNKS = 4
Y_ORDER = (2, 1, 3)
SERVED = (2, 1, 7)
AHEAD = 4
MESH = pl.DeviceIdType.MESH
F32 = jnp.float32
BF = jnp.bfloat16


def dot(a, b):
    return lax.dot_general(a, b, (((1,), (0,)), ((), ())), preferred_element_type=F32)


def dot_nt(a, b):
    return lax.dot_general(a, b, (((1,), (1,)), ((), ())), preferred_element_type=F32)


def dot_tn(a, b):
    return lax.dot_general(a, b, (((0,), (0,)), ((), ())), preferred_element_type=F32)


def each(lo, hi, fn):
    def step(i, carry):
        fn(i)
        return carry

    lax.fori_loop(lo, hi, step, 0)


def far_first(n):
    return sorted(range(1, n), key=lambda d: -min(d, n - d))


def store_kernel(*refs):
    sem = refs[10]
    copies = [pltpu.make_async_copy(refs[i], refs[5 + i], sem.at[i]) for i in range(5)]
    for cp in copies:
        cp.start()
    for cp in copies:
        cp.wait()


def layer_kernel(
    nz,
    nh,
    heads,
    rows,
    full,
    q_hbm,
    k_hbm,
    v_hbm,
    gate_hbm,
    go_hbm,
    gain_hbm,
    tm_hbm,
    gq,
    gk,
    gv,
    gg,
    gg_sum_ref,
    q,
    k,
    v,
    gate,
    go,
    attn,
    dg,
    da,
    gk_in,
    gv_in,
    mask,
    mask_t,
    probs_t,
    dn,
    slope,
    acc_sq,
    acc_cr,
    rb,
    cb,
    st,
    r1,
    tb,
    r2,
    xb,
    r3,
    pb,
    pr,
    prefb,
    sb,
    hr,
    gp,
    gr1,
    gt,
    gr2,
    gain_ref,
    tm_ref,
    in_sem,
    kv_sem,
    sent,
    came,
    x_sent,
    x_came,
):
    seq = lax.axis_index("seq")
    head = lax.axis_index("head")
    z = seq // NY
    y = lax.rem(seq, NY)
    per = heads // CHUNKS
    crow = per * HD
    prow = crow // NY
    zrow = prow // (nz // 2)

    def cols(h):
        return pl.ds(pl.multiple_of(h * HD, HD), HD)

    def ypeer(d):
        yp = lax.rem(y + d, NY)
        return yp, (z * NY + yp, head)

    def zpeer(d):
        zp = lax.rem(z + d, nz)
        return zp, (zp * NY + y, head)

    def hpeer(d):
        return (seq, lax.rem(head + d, nh))

    def rcopy(src, dst, ss, rs, dev):
        return pltpu.make_async_remote_copy(
            src_ref=src, dst_ref=dst, send_sem=ss, recv_sem=rs, device_id=dev, device_id_type=MESH
        )

    bar = pltpu.get_barrier_semaphore()

    def greet(dev):
        pl.semaphore_signal(bar, inc=1, device_id=dev, device_id_type=MESH)

    each(1, NY, lambda d: greet(ypeer(d)[1]))
    each(1, nz, lambda d: greet(zpeer(d)[1]))
    each(1, nh, lambda d: greet(hpeer(d)))

    def kv_copy(c, i):
        src, dst = ((k_hbm, k), (v_hbm, v))[i]
        w = pl.ds(c * crow, crow)
        return pltpu.make_async_copy(src.at[:, w], dst.at[:, w], kv_sem.at[c, i])

    for c in range(CHUNKS):
        kv_copy(c, 0).start()
        kv_copy(c, 1).start()
    pairs = ((tm_hbm, tm_ref), (gain_hbm, gain_ref), (q_hbm, q), (go_hbm, go), (gate_hbm, gate))
    loads = [
        pltpu.make_async_copy(a, b, in_sem.at[i])
        for i, (a, b) in enumerate(pairs)
    ]
    for cp in loads:
        cp.start()

    def settle(ref, sem):
        pltpu.make_async_copy(ref, ref, sem).wait()

    def share(i):
        return pl.ds(pl.multiple_of(lax.rem(i, nz // 2) * zrow, 8), zrow)

    def p1(s, c, d):
        yp, dev = ypeer(d)
        src = st.at[s, pl.ds(pl.multiple_of(c * crow + yp * prow, 8), prow)]
        return rcopy(src, r1.at[s, c, y], sent.at[s, 0], came.at[s, 0, c], dev)

    def p2(s, c, d):
        zp, dev = zpeer(d)
        src = tb.at[s, c, share(zp)]
        return rcopy(src, r2.at[s, c, z], sent.at[s, 1], came.at[s, 1, c], dev)

    def p3(s, c, d):
        zp, dev = zpeer(d)
        dst = r3.at[s, c, share(z)]
        return rcopy(xb.at[s, c, zp], dst, sent.at[s, 2], came.at[s, 2, c], dev)

    def p4(s, c, d):
        yp, dev = ypeer(d)
        dst = pr.at[s, pl.ds(pl.multiple_of(c * crow + y * prow, 8), prow)]
        return rcopy(pb.at[s, c, yp], dst, sent.at[s, 3], came.at[s, 3, c], dev)

    def start_p1(s, c):
        own = st[s, pl.ds(pl.multiple_of(c * crow + y * prow, 8), prow)]
        for d in Y_ORDER:
            p1(s, c, d).start()
        r1[s, c, y] = own

    def step_a(s, c):
        settle(r1.at[s, c, 0 : NY - 1], came.at[s, 0, c])
        t = r1[s, c, 0]
        for i in range(1, NY):
            t = t + r1[s, c, i]
        tb[s, c] = t
        for d in far_first(nz):
            p2(s, c, d).start()
        r2[s, c, z] = tb[s, c, share(z)]

    def step_b(s, c):
        settle(r2.at[s, c, 0 : nz - 1], came.at[s, 1, c])
        x = jnp.zeros((zrow, HD), F32)
        for i in range(nz) if s == 0 else reversed(range(nz)):
            xb[s, c, i] = x
            x = x + r2[s, c, i]
        for d in SERVED:
            p3(s, c, d).start()
        r3[s, c, share(z)] = xb[s, c, z]

    def step_c(s, c):
        settle(r3.at[s, c, 0 : len(SERVED) * zrow], came.at[s, 2, c])
        x = r3[s, c]
        for i in range(NY) if s == 0 else reversed(range(NY)):
            pb[s, c, i] = x
            x = x + r1[s, c, i]
        for d in Y_ORDER:
            p4(s, c, d).start()
        pr[s, pl.ds(pl.multiple_of(c * crow + y * prow, 8), prow)] = pb[s, c, y]

    def wait_d(s, c):
        settle(pr.at[s, 0 : (NY - 1) * prow], came.at[s, 3, c])

    def wait_sends(s):
        settle(st.at[s, 0 : CHUNKS * (NY - 1) * prow], sent.at[s, 0])
        settle(r2.at[s, :, 0 : nz - 1], sent.at[s, 1])
        settle(xb.at[s, :, 0 : len(SERVED)], sent.at[s, 2])
        settle(pb.at[s, :, 0 : NY - 1], sent.at[s, 3])

    def state(c):
        def one(h):
            w = cols(h)
            st[0, pl.ds(pl.multiple_of(h * HD, HD), HD)] = dot_tn(k[:, w], v[:, w])

        each(c * per, (c + 1) * per, one)

    for c in range(CHUNKS):
        kv_copy(c, 0).wait()
        kv_copy(c, 1).wait()
        state(c)

    loads[0].wait()
    tiles = rows // TILE
    at_row = lax.broadcasted_iota(jnp.int32, (TILE, TILE), 0)
    at_col = lax.broadcasted_iota(jnp.int32, (TILE, TILE), 1)
    for i in range(tiles):
        for j in range(tiles):
            on = jnp.broadcast_to(tm_ref[i : i + 1, j : j + 1], (TILE, TILE)) == 1
            low = on & (at_row >= at_col) if i == j else on
            high = on & (at_col >= at_row) if i == j else on
            ri, cj = pl.ds(i * TILE, TILE), pl.ds(j * TILE, TILE)
            mask[ri, cj] = jnp.where(low, 1.0, 0.0).astype(BF)
            mask_t[cj, ri] = jnp.where(high, 1.0, 0.0).astype(BF)

    pl.semaphore_wait(bar, NY + nz + nh - 3)
    each(0, CHUNKS, lambda c: start_p1(0, c))

    for cp in loads[1:]:
        cp.wait()

    half = rows // 2
    lower = ((0, half, half), (half, half, rows))
    upper = ((0, half, 0, rows), (half, half, half, half))

    def fwd(h):
        w = cols(h)
        for r0, rn, cn in lower:
            sc = dot_nt(q[r0 : r0 + rn, w], k[0:cn, w])
            p = sc.astype(BF) * mask[r0 : r0 + rn, 0:cn]
            attn[r0 : r0 + rn, w] = dot(p, v[0:cn, w])

    def gated(h):
        w = cols(h)
        sig = jax.nn.sigmoid(gate[:, w].astype(F32))
        d = go[:, w].astype(F32) * sig
        g = d * gain_ref[:, w]
        dn[:, w] = d
        dg[:, w] = g
        slope[:, w] = g * (1.0 - sig)

    def turned(h):
        w = cols(h)
        for r0, rn, c0, cn in upper:
            pp = dot_nt(k[r0 : r0 + rn, w], q[c0 : c0 + cn, w]).astype(BF)
            probs_t[h, r0 : r0 + rn, c0 : c0 + cn] = pp * mask_t[r0 : r0 + rn, c0 : c0 + cn]

    def finish_attn(h):
        w = cols(h)
        pf = pr[0, pl.ds(pl.multiple_of(h * HD, HD), HD)].astype(BF)
        prefb[h] = pf
        a = attn[:, w] + dot(q[:, w], pf)
        attn[:, w] = a
        acc_sq[...] += a * a
        acc_cr[...] += dg[:, w] * a

    acc_sq[...] = jnp.zeros_like(acc_sq)
    acc_cr[...] = jnp.zeros_like(acc_cr)

    def during(i, lo, n, fn):
        @pl.when((i >= lo) & (i < lo + n))
        def _():
            fn(i - lo)

    def close1(c):
        wait_d(0, c)
        each(c * per, (c + 1) * per, finish_attn)

    def scan1(i):
        during(i, 0, CHUNKS, lambda c: step_a(0, c))
        during(i, CHUNKS - 1, CHUNKS, lambda c: step_b(0, c))
        during(i, 2 * CHUNKS - 2, CHUNKS, lambda c: step_c(0, c))
        during(i, 0, heads - AHEAD, lambda h: fwd(AHEAD + h))
        during(i, 0, heads, gated)
        during(i, 0, heads, turned)
        during(i, 2 * CHUNKS + 2, CHUNKS, close1)

    each(0, AHEAD, fwd)
    each(0, 3 * CHUNKS + 2, scan1)

    eye = jnp.where(at_row == at_col, 1.0, 0.0)
    for i in range(tiles):
        ri = slice(i * TILE, (i + 1) * TILE)
        for n, acc in ((i, acc_sq), (tiles + i, acc_cr)):
            total = jnp.sum(acc[ri], axis=1, keepdims=True)
            sb[n : n + 1] = jnp.sum(total * eye, axis=0, keepdims=True)

    def hx(d):
        return rcopy(sb, hr.at[head], x_sent.at[0], x_came.at[0], hpeer(d))

    for d in far_first(nh):
        hx(d).start()
    hr[head] = sb[...]
    settle(hr.at[0 : nh - 1], x_came.at[0])
    tot = hr[0]
    for i in range(1, nh):
        tot = tot + hr[i]
    ms = tot[0:tiles] * (1.0 / full) + 1e-06
    inv = 1.0 / jnp.sqrt(ms)
    cross = tot[tiles : 2 * tiles] * (1.0 / full) / ms * inv
    for i in range(tiles):
        ri = slice(i * TILE, (i + 1) * TILE)
        for line, wide in ((inv, rb), (cross, cb)):
            col = jnp.sum(line[i : i + 1] * eye, axis=1, keepdims=True)
            wide[ri] = jnp.broadcast_to(col, (TILE, HD))

    def adjoint(h):
        w = cols(h)
        d = (dg[:, w] * rb[...] - attn[:, w] * cb[...]).astype(BF)
        da[:, w] = d
        st[1, pl.ds(pl.multiple_of(h * HD, HD), HD)] = dot_tn(q[:, w], d)

    def adj_chunk(c):
        each(c * per, (c + 1) * per, adjoint)
        start_p1(1, c)

    each(0, CHUNKS, adj_chunk)

    def gates(h):
        w = cols(h)
        norm = attn[:, w] * rb[...]
        gg[:, w] = (norm * slope[:, w]).astype(BF)
        gp[pl.ds(h, 1)] = jnp.sum(dn[:, w] * norm, axis=0, keepdims=True)

    def bwd(h):
        w = cols(h)
        for r0, rn, cn in lower:
            d = da[r0 : r0 + rn, w]
            dp = dot_nt(d, v[0:cn, w]).astype(BF) * mask[r0 : r0 + rn, 0:cn]
            gq[r0 : r0 + rn, w] = (dot(dp, k[0:cn, w]) + dot_nt(d, prefb[h])).astype(BF)
        for r0, rn, c0, cn in upper:
            d = da[c0 : c0 + cn, w]
            m = mask_t[r0 : r0 + rn, c0 : c0 + cn]
            dp = dot_nt(v[r0 : r0 + rn, w], d).astype(BF) * m
            gk_in[r0 : r0 + rn, w] = dot(dp, q[c0 : c0 + cn, w])
            gv_in[r0 : r0 + rn, w] = dot(probs_t[h, r0 : r0 + rn, c0 : c0 + cn], d)

    def finish(h):
        w = cols(h)
        sf = pr[1, pl.ds(pl.multiple_of(h * HD, HD), HD)].astype(BF)
        gk[:, w] = (gk_in[:, w] + dot_nt(v[:, w], sf)).astype(BF)
        gv[:, w] = (gv_in[:, w] + dot(k[:, w], sf)).astype(BF)

    def gx1(d):
        return rcopy(gp, gr1.at[y], x_sent.at[1], x_came.at[1], ypeer(d)[1])

    def gx2(d):
        return rcopy(gt, gr2.at[z], x_sent.at[2], x_came.at[2], zpeer(d)[1])

    def close2(c):
        wait_d(1, c)
        each(c * per, (c + 1) * per, finish)

    def scan2(i):
        during(i, 0, CHUNKS, lambda c: step_a(1, c))
        during(i, CHUNKS - 1, CHUNKS, lambda c: step_b(1, c))
        during(i, 2 * CHUNKS - 2, CHUNKS, lambda c: step_c(1, c))

        @pl.when(i == CHUNKS - 1)
        def _():
            each(heads // 2, heads, gates)
            each(1, NY, lambda d: gx1(d).start())
            gr1[y] = gp[...]

        @pl.when(i == 2 * CHUNKS)
        def _():
            settle(gr1.at[0 : NY - 1], x_came.at[1])
            t = gr1[0]
            for n in range(1, NY):
                t = t + gr1[n]
            gt[...] = t
            each(1, nz, lambda d: gx2(d).start())
            gr2[z] = t

        @pl.when((i < heads) & (i != CHUNKS - 1))
        def _():
            bwd(jnp.where(i < CHUNKS - 1, i + 1, i))

        during(i, 2 * CHUNKS + 2, CHUNKS, close2)

    each(0, heads // 2, gates)
    bwd(0)
    each(0, 3 * CHUNKS + 2, scan2)

    settle(gr2.at[0 : nz - 1], x_came.at[2])
    t = gr2[0]
    for n in range(1, nz):
        t = t + gr2[n]
    gg_sum_ref[...] = t

    wait_sends(0)
    wait_sends(1)
    settle(hr.at[0 : nh - 1], x_sent.at[0])
    settle(gr1.at[0 : NY - 1], x_sent.at[1])
    settle(gr2.at[0 : nz - 1], x_sent.at[2])


def body(nz, nh, queries, keys, values, gate, grad_out, gain, tile_mask):
    rows, width = queries.shape
    heads = width // HD
    full = width * nh
    per = heads // CHUNKS
    crow = per * HD
    prow = crow // NY
    zrow = prow // (nz // 2)
    dma = pltpu.SemaphoreType.DMA
    vm = pltpu.VMEM
    big = jax.ShapeDtypeStruct((rows, width), BF)
    scratch = (
        [vm((rows, width), BF)] * 5
        + [vm((rows, width), F32)] * 2
        + [vm((rows, width), BF)]
        + [vm((rows, width), F32)] * 2
        + [vm((rows, rows), BF)] * 2
        + [vm((heads, rows, rows), BF)]
        + [vm((rows, width), F32)] * 2
        + [vm((rows, HD), F32)] * 4
        + [
            vm((2, heads * HD, HD), F32),
            vm((2, CHUNKS, NY, prow, HD), F32),
            vm((2, CHUNKS, prow, HD), F32),
            vm((2, CHUNKS, nz, zrow, HD), F32),
            vm((2, CHUNKS, nz, zrow, HD), F32),
            vm((2, CHUNKS, prow, HD), F32),
            vm((2, CHUNKS, NY, prow, HD), F32),
            vm((2, heads * HD, HD), F32),
            vm((heads, HD, HD), BF),
            vm((8, HD), F32),
            vm((nh, 8, HD), F32),
            vm((heads, HD), F32),
            vm((NY, heads, HD), F32),
            vm((heads, HD), F32),
            vm((nz, heads, HD), F32),
            vm((1, width), F32),
            vm(tile_mask.shape, jnp.int32),
            dma((5,)),
            dma((CHUNKS, 2)),
            dma((2, 4)),
            dma((2, 4, CHUNKS)),
            dma((3,)),
            dma((3,)),
        ]
    )
    hbm = pl.BlockSpec(memory_space=pl.ANY)
    args = (queries, keys, values, gate, grad_out, gain.reshape(1, width), tile_mask)
    parts = pl.pallas_call(
        functools.partial(layer_kernel, nz, nh, heads, rows, full),
        out_shape=(big, big, big, big, jax.ShapeDtypeStruct((heads, HD), F32)),
        in_specs=[hbm] * 7,
        out_specs=(pl.BlockSpec(memory_space=pltpu.VMEM),) * 5,
        scratch_shapes=scratch,
        compiler_params=pltpu.CompilerParams(
            collective_id=0, has_side_effects=True, vmem_limit_bytes=44 * 1024 * 1024
        ),
        name="layer",
    )(*(pltpu.with_memory_space_constraint(a, pltpu.HBM) for a in args))
    out = pl.pallas_call(
        store_kernel,
        out_shape=(big, big, big, big, jax.ShapeDtypeStruct((heads, HD), F32)),
        in_specs=[pl.BlockSpec(memory_space=pltpu.VMEM)] * 5,
        out_specs=(hbm,) * 5,
        scratch_shapes=[dma((5,))],
        compiler_params=pltpu.CompilerParams(vmem_limit_bytes=8 * 1024 * 1024),
        name="store",
    )(*parts)
    return out[0], out[1], out[2], out[3], out[4].reshape(width)


def solution(mesh):
    nz = mesh.shape["seq"] // NY
    nh = mesh.shape["head"]
    wide = P("seq", "head")
    return jax.shard_map(
        functools.partial(body, nz, nh),
        mesh=mesh,
        in_specs=(wide, wide, wide, wide, wide, P("head"), P("seq", None)),
        out_specs=(wide, wide, wide, wide, P("head")),
        check_vma=False,
    )
```

```python
import functools

import jax
import jax.numpy as jnp
from jax import lax
from jax.experimental import pallas as pl
from jax.experimental.pallas import tpu as pltpu
from jax.sharding import PartitionSpec as P

HD = 128
TILE = 128
NY = 4
CHUNKS = 4
Y_ORDER = (2, 1, 3)
SERVED = (2, 1, 7)
AHEAD = 4
MESH = pl.DeviceIdType.MESH
F32 = jnp.float32
BF = jnp.bfloat16


def dot(a, b):
    return lax.dot_general(a, b, (((1,), (0,)), ((), ())), preferred_element_type=F32)


def dot_nt(a, b):
    return lax.dot_general(a, b, (((1,), (1,)), ((), ())), preferred_element_type=F32)


def dot_tn(a, b):
    return lax.dot_general(a, b, (((0,), (0,)), ((), ())), preferred_element_type=F32)


def each(lo, hi, fn):
    def step(i, carry):
        fn(i)
        return carry

    lax.fori_loop(lo, hi, step, 0)


def far_first(n):
    return sorted(range(1, n), key=lambda d: -min(d, n - d))


def store_kernel(*refs):
    sem = refs[10]
    copies = [pltpu.make_async_copy(refs[i], refs[5 + i], sem.at[i]) for i in range(5)]
    for cp in copies:
        cp.start()
    for cp in copies:
        cp.wait()


def layer_kernel(
    nz,
    nh,
    heads,
    rows,
    full,
    q_hbm,
    k_hbm,
    v_hbm,
    gate_hbm,
    go_hbm,
    gain_hbm,
    tm_hbm,
    gq,
    gk,
    gv,
    gg,
    gg_sum_ref,
    q,
    k,
    v,
    gate,
    go,
    attn,
    dg,
    da,
    gk_in,
    gv_in,
    mask,
    mask_t,
    probs_t,
    dn,
    slope,
    acc_sq,
    acc_cr,
    rb,
    cb,
    st,
    r1,
    tb,
    r2,
    xb,
    r3,
    pb,
    pr,
    prefb,
    sb,
    hr,
    gp,
    gr1,
    gt,
    gr2,
    gain_ref,
    tm_ref,
    in_sem,
    kv_sem,
    sent,
    came,
    x_sent,
    x_came,
):
    seq = lax.axis_index("seq")
    head = lax.axis_index("head")
    z = seq // NY
    y = lax.rem(seq, NY)
    per = heads // CHUNKS
    crow = per * HD
    prow = crow // NY
    zrow = prow // (nz // 2)

    def cols(h):
        return pl.ds(pl.multiple_of(h * HD, HD), HD)

    def ypeer(d):
        yp = lax.rem(y + d, NY)
        return yp, (z * NY + yp, head)

    def zpeer(d):
        zp = lax.rem(z + d, nz)
        return zp, (zp * NY + y, head)

    def hpeer(d):
        return (seq, lax.rem(head + d, nh))

    def rcopy(src, dst, ss, rs, dev):
        return pltpu.make_async_remote_copy(
            src_ref=src, dst_ref=dst, send_sem=ss, recv_sem=rs, device_id=dev, device_id_type=MESH
        )

    bar = pltpu.get_barrier_semaphore()

    def greet(dev):
        pl.semaphore_signal(bar, inc=1, device_id=dev, device_id_type=MESH)

    for d in far_first(nz):
        greet(zpeer(d)[1])
    for d in Y_ORDER:
        greet(ypeer(d)[1])
    for d in far_first(nh):
        greet(hpeer(d))

    def kv_copy(c, i):
        src, dst = ((k_hbm, k), (v_hbm, v))[i]
        w = pl.ds(c * crow, crow)
        return pltpu.make_async_copy(src.at[:, w], dst.at[:, w], kv_sem.at[c, i])

    for c in range(CHUNKS):
        kv_copy(c, 0).start()
        kv_copy(c, 1).start()
    pairs = ((tm_hbm, tm_ref), (gain_hbm, gain_ref), (q_hbm, q), (go_hbm, go), (gate_hbm, gate))
    loads = [
        pltpu.make_async_copy(a, b, in_sem.at[i])
        for i, (a, b) in enumerate(pairs)
    ]
    for cp in loads:
        cp.start()

    def settle(ref, sem):
        pltpu.make_async_copy(ref, ref, sem).wait()

    def share(i):
        return pl.ds(pl.multiple_of(lax.rem(i, nz // 2) * zrow, 8), zrow)

    def p1(s, c, d):
        yp, dev = ypeer(d)
        src = st.at[s, pl.ds(pl.multiple_of(c * crow + yp * prow, 8), prow)]
        return rcopy(src, r1.at[s, c, y], sent.at[s, 0], came.at[s, 0, c], dev)

    def p2(s, c, d):
        zp, dev = zpeer(d)
        src = tb.at[s, c, share(zp)]
        return rcopy(src, r2.at[s, c, z], sent.at[s, 1], came.at[s, 1, c], dev)

    def p3(s, c, d):
        zp, dev = zpeer(d)
        dst = r3.at[s, c, share(z)]
        return rcopy(xb.at[s, c, zp], dst, sent.at[s, 2], came.at[s, 2, c], dev)

    def p4(s, c, d):
        yp, dev = ypeer(d)
        dst = pr.at[s, pl.ds(pl.multiple_of(c * crow + y * prow, 8), prow)]
        return rcopy(pb.at[s, c, yp], dst, sent.at[s, 3], came.at[s, 3, c], dev)

    def start_p1(s, c):
        own = st[s, pl.ds(pl.multiple_of(c * crow + y * prow, 8), prow)]
        for d in Y_ORDER:
            p1(s, c, d).start()
        r1[s, c, y] = own

    def step_a(s, c):
        settle(r1.at[s, c, 0 : NY - 1], came.at[s, 0, c])
        t = r1[s, c, 0]
        for i in range(1, NY):
            t = t + r1[s, c, i]
        tb[s, c] = t
        for d in far_first(nz):
            p2(s, c, d).start()
        r2[s, c, z] = tb[s, c, share(z)]

    def step_b(s, c):
        settle(r2.at[s, c, 0 : nz - 1], came.at[s, 1, c])
        x = jnp.zeros((zrow, HD), F32)
        for i in range(nz) if s == 0 else reversed(range(nz)):
            xb[s, c, i] = x
            x = x + r2[s, c, i]
        for d in SERVED:
            p3(s, c, d).start()
        r3[s, c, share(z)] = xb[s, c, z]

    def step_c(s, c):
        settle(r3.at[s, c, 0 : len(SERVED) * zrow], came.at[s, 2, c])
        x = r3[s, c]
        for i in range(NY) if s == 0 else reversed(range(NY)):
            pb[s, c, i] = x
            x = x + r1[s, c, i]
        for d in Y_ORDER:
            p4(s, c, d).start()
        pr[s, pl.ds(pl.multiple_of(c * crow + y * prow, 8), prow)] = pb[s, c, y]

    def wait_d(s, c):
        settle(pr.at[s, 0 : (NY - 1) * prow], came.at[s, 3, c])

    def wait_sends(s):
        settle(st.at[s, 0 : CHUNKS * (NY - 1) * prow], sent.at[s, 0])
        settle(r2.at[s, :, 0 : nz - 1], sent.at[s, 1])
        settle(xb.at[s, :, 0 : len(SERVED)], sent.at[s, 2])
        settle(pb.at[s, :, 0 : NY - 1], sent.at[s, 3])

    def state(c):
        def one(h):
            w = cols(h)
            st[0, pl.ds(pl.multiple_of(h * HD, HD), HD)] = dot_tn(k[:, w], v[:, w])

        each(c * per, (c + 1) * per, one)

    for c in range(CHUNKS):
        kv_copy(c, 0).wait()
        kv_copy(c, 1).wait()
        state(c)

    loads[0].wait()
    tiles = rows // TILE
    at_row = lax.broadcasted_iota(jnp.int32, (TILE, TILE), 0)
    at_col = lax.broadcasted_iota(jnp.int32, (TILE, TILE), 1)
    for i in range(tiles):
        for j in range(tiles):
            on = jnp.broadcast_to(tm_ref[i : i + 1, j : j + 1], (TILE, TILE)) == 1
            low = on & (at_row >= at_col) if i == j else on
            high = on & (at_col >= at_row) if i == j else on
            ri, cj = pl.ds(i * TILE, TILE), pl.ds(j * TILE, TILE)
            mask[ri, cj] = jnp.where(low, 1.0, 0.0).astype(BF)
            mask_t[cj, ri] = jnp.where(high, 1.0, 0.0).astype(BF)

    pl.semaphore_wait(bar, NY + nz + nh - 3)
    each(0, CHUNKS, lambda c: start_p1(0, c))

    for cp in loads[1:]:
        cp.wait()

    half = rows // 2
    lower = ((0, half, half), (half, half, rows))
    upper = ((0, half, 0, rows), (half, half, half, half))

    def fwd(h):
        w = cols(h)
        for r0, rn, cn in lower:
            sc = dot_nt(q[r0 : r0 + rn, w], k[0:cn, w])
            p = sc.astype(BF) * mask[r0 : r0 + rn, 0:cn]
            attn[r0 : r0 + rn, w] = dot(p, v[0:cn, w])

    def gated(h):
        w = cols(h)
        sig = jax.nn.sigmoid(gate[:, w].astype(F32))
        d = go[:, w].astype(F32) * sig
        g = d * gain_ref[:, w]
        dn[:, w] = d
        dg[:, w] = g
        slope[:, w] = g * (1.0 - sig)

    def turned(h):
        w = cols(h)
        for r0, rn, c0, cn in upper:
            pp = dot_nt(k[r0 : r0 + rn, w], q[c0 : c0 + cn, w]).astype(BF)
            probs_t[h, r0 : r0 + rn, c0 : c0 + cn] = pp * mask_t[r0 : r0 + rn, c0 : c0 + cn]

    def finish_attn(h):
        w = cols(h)
        pf = pr[0, pl.ds(pl.multiple_of(h * HD, HD), HD)].astype(BF)
        prefb[h] = pf
        a = attn[:, w] + dot(q[:, w], pf)
        attn[:, w] = a
        acc_sq[...] += a * a
        acc_cr[...] += dg[:, w] * a

    acc_sq[...] = jnp.zeros_like(acc_sq)
    acc_cr[...] = jnp.zeros_like(acc_cr)

    def during(i, lo, n, fn):
        @pl.when((i >= lo) & (i < lo + n))
        def _():
            fn(i - lo)

    def close1(c):
        wait_d(0, c)
        for n in range(per):
            finish_attn(c * per + n)

    def scan1(i):
        during(i, 0, CHUNKS, lambda c: step_a(0, c))
        during(i, CHUNKS - 1, CHUNKS, lambda c: step_b(0, c))
        during(i, 2 * CHUNKS - 2, CHUNKS, lambda c: step_c(0, c))
        during(i, 0, heads - AHEAD, lambda h: fwd(AHEAD + h))
        during(i, 0, heads, gated)
        during(i, 0, heads, turned)
        during(i, 2 * CHUNKS + 2, CHUNKS, close1)

    each(0, AHEAD, fwd)
    each(0, 3 * CHUNKS + 2, scan1)

    eye = jnp.where(at_row == at_col, 1.0, 0.0)
    for i in range(tiles):
        ri = slice(i * TILE, (i + 1) * TILE)
        for n, acc in ((i, acc_sq), (tiles + i, acc_cr)):
            total = jnp.sum(acc[ri], axis=1, keepdims=True)
            sb[n : n + 1] = jnp.sum(total * eye, axis=0, keepdims=True)

    def hx(d):
        return rcopy(sb, hr.at[head], x_sent.at[0], x_came.at[0], hpeer(d))

    for d in far_first(nh):
        hx(d).start()
    hr[head] = sb[...]
    settle(hr.at[0 : nh - 1], x_came.at[0])
    tot = hr[0]
    for i in range(1, nh):
        tot = tot + hr[i]
    ms = tot[0:tiles] * (1.0 / full) + 1e-06
    inv = 1.0 / jnp.sqrt(ms)
    cross = tot[tiles : 2 * tiles] * (1.0 / full) / ms * inv
    for i in range(tiles):
        ri = slice(i * TILE, (i + 1) * TILE)
        for line, wide in ((inv, rb), (cross, cb)):
            col = jnp.sum(line[i : i + 1] * eye, axis=1, keepdims=True)
            wide[ri] = jnp.broadcast_to(col, (TILE, HD))

    def adjoint(h):
        w = cols(h)
        d = (dg[:, w] * rb[...] - attn[:, w] * cb[...]).astype(BF)
        da[:, w] = d
        st[1, pl.ds(pl.multiple_of(h * HD, HD), HD)] = dot_tn(q[:, w], d)

    def adj_chunk(c):
        for n in range(per):
            adjoint(c * per + n)
        start_p1(1, c)

    each(0, CHUNKS, adj_chunk)

    def gates(h):
        w = cols(h)
        norm = attn[:, w] * rb[...]
        gg[:, w] = (norm * slope[:, w]).astype(BF)
        gp[pl.ds(h, 1)] = jnp.sum(dn[:, w] * norm, axis=0, keepdims=True)

    def bwd(h):
        w = cols(h)
        for r0, rn, cn in lower:
            d = da[r0 : r0 + rn, w]
            dp = dot_nt(d, v[0:cn, w]).astype(BF) * mask[r0 : r0 + rn, 0:cn]
            gq[r0 : r0 + rn, w] = (dot(dp, k[0:cn, w]) + dot_nt(d, prefb[h])).astype(BF)
        for r0, rn, c0, cn in upper:
            d = da[c0 : c0 + cn, w]
            m = mask_t[r0 : r0 + rn, c0 : c0 + cn]
            dp = dot_nt(v[r0 : r0 + rn, w], d).astype(BF) * m
            gk_in[r0 : r0 + rn, w] = dot(dp, q[c0 : c0 + cn, w])
            gv_in[r0 : r0 + rn, w] = dot(probs_t[h, r0 : r0 + rn, c0 : c0 + cn], d)

    def finish(h):
        w = cols(h)
        sf = pr[1, pl.ds(pl.multiple_of(h * HD, HD), HD)].astype(BF)
        gk[:, w] = (gk_in[:, w] + dot_nt(v[:, w], sf)).astype(BF)
        gv[:, w] = (gv_in[:, w] + dot(k[:, w], sf)).astype(BF)

    def gx1(d):
        return rcopy(gp, gr1.at[y], x_sent.at[1], x_came.at[1], ypeer(d)[1])

    def gx2(d):
        return rcopy(gt, gr2.at[z], x_sent.at[2], x_came.at[2], zpeer(d)[1])

    def close2(c):
        wait_d(1, c)
        for n in range(per):
            finish(c * per + n)

    def scan2(i):
        during(i, 0, CHUNKS, lambda c: step_a(1, c))
        during(i, CHUNKS - 1, CHUNKS, lambda c: step_b(1, c))
        during(i, 2 * CHUNKS - 2, CHUNKS, lambda c: step_c(1, c))

        @pl.when(i == CHUNKS - 1)
        def _():
            each(heads // 2, heads, gates)
            each(1, NY, lambda d: gx1(d).start())
            gr1[y] = gp[...]

        @pl.when(i == 2 * CHUNKS)
        def _():
            settle(gr1.at[0 : NY - 1], x_came.at[1])
            t = gr1[0]
            for n in range(1, NY):
                t = t + gr1[n]
            gt[...] = t
            each(1, nz, lambda d: gx2(d).start())
            gr2[z] = t

        @pl.when((i < heads) & (i != CHUNKS - 1))
        def _():
            bwd(jnp.where(i < CHUNKS - 1, i + 1, i))

        during(i, 2 * CHUNKS + 2, CHUNKS, close2)

    each(0, heads // 2, gates)
    bwd(0)
    each(0, 3 * CHUNKS + 2, scan2)

    settle(gr2.at[0 : nz - 1], x_came.at[2])
    t = gr2[0]
    for n in range(1, nz):
        t = t + gr2[n]
    gg_sum_ref[...] = t

    wait_sends(0)
    wait_sends(1)
    settle(hr.at[0 : nh - 1], x_sent.at[0])
    settle(gr1.at[0 : NY - 1], x_sent.at[1])
    settle(gr2.at[0 : nz - 1], x_sent.at[2])


def body(nz, nh, queries, keys, values, gate, grad_out, gain, tile_mask):
    rows, width = queries.shape
    heads = width // HD
    full = width * nh
    per = heads // CHUNKS
    crow = per * HD
    prow = crow // NY
    zrow = prow // (nz // 2)
    dma = pltpu.SemaphoreType.DMA
    vm = pltpu.VMEM
    big = jax.ShapeDtypeStruct((rows, width), BF)
    scratch = (
        [vm((rows, width), BF)] * 5
        + [vm((rows, width), F32)] * 2
        + [vm((rows, width), BF)]
        + [vm((rows, width), F32)] * 2
        + [vm((rows, rows), BF)] * 2
        + [vm((heads, rows, rows), BF)]
        + [vm((rows, width), F32)] * 2
        + [vm((rows, HD), F32)] * 4
        + [
            vm((2, heads * HD, HD), F32),
            vm((2, CHUNKS, NY, prow, HD), F32),
            vm((2, CHUNKS, prow, HD), F32),
            vm((2, CHUNKS, nz, zrow, HD), F32),
            vm((2, CHUNKS, nz, zrow, HD), F32),
            vm((2, CHUNKS, prow, HD), F32),
            vm((2, CHUNKS, NY, prow, HD), F32),
            vm((2, heads * HD, HD), F32),
            vm((heads, HD, HD), BF),
            vm((8, HD), F32),
            vm((nh, 8, HD), F32),
            vm((heads, HD), F32),
            vm((NY, heads, HD), F32),
            vm((heads, HD), F32),
            vm((nz, heads, HD), F32),
            vm((1, width), F32),
            vm(tile_mask.shape, jnp.int32),
            dma((5,)),
            dma((CHUNKS, 2)),
            dma((2, 4)),
            dma((2, 4, CHUNKS)),
            dma((3,)),
            dma((3,)),
        ]
    )
    hbm = pl.BlockSpec(memory_space=pl.ANY)
    args = (queries, keys, values, gate, grad_out, gain.reshape(1, width), tile_mask)
    parts = pl.pallas_call(
        functools.partial(layer_kernel, nz, nh, heads, rows, full),
        out_shape=(big, big, big, big, jax.ShapeDtypeStruct((heads, HD), F32)),
        in_specs=[hbm] * 7,
        out_specs=(pl.BlockSpec(memory_space=pltpu.VMEM),) * 5,
        scratch_shapes=scratch,
        compiler_params=pltpu.CompilerParams(
            collective_id=0, has_side_effects=True, vmem_limit_bytes=44 * 1024 * 1024
        ),
        name="layer",
    )(*(pltpu.with_memory_space_constraint(a, pltpu.HBM) for a in args))
    out = pl.pallas_call(
        store_kernel,
        out_shape=(big, big, big, big, jax.ShapeDtypeStruct((heads, HD), F32)),
        in_specs=[pl.BlockSpec(memory_space=pltpu.VMEM)] * 5,
        out_specs=(hbm,) * 5,
        scratch_shapes=[dma((5,))],
        compiler_params=pltpu.CompilerParams(vmem_limit_bytes=8 * 1024 * 1024),
        name="store",
    )(*parts)
    return out[0], out[1], out[2], out[3], out[4].reshape(width)


def solution(mesh):
    nz = mesh.shape["seq"] // NY
    nh = mesh.shape["head"]
    wide = P("seq", "head")
    return jax.shard_map(
        functools.partial(body, nz, nh),
        mesh=mesh,
        in_specs=(wide, wide, wide, wide, wide, P("head"), P("seq", None)),
        out_specs=(wide, wide, wide, wide, P("head")),
        check_vma=False,
    )
```
